512 devices in a mesh: vol: 64 (over z, x, y_hi), path: 8 (over y_lo, core).
Axes of the slice: x: 4, y: 8 (y_hi: 2, y_lo: 4; y = y_hi * 4 + y_lo), z: 8, core: 2. Of those that a mesh axis runs over, the one named last changes fastest.
Arguments:
- factors: bfloat16 [16, 8192], P(None, 'path'), may hold values from -6 to 6
- payoff: float32 [4, 8192], P(None, 'path'), may hold values from -6 to 6
- terminal: float32 [64, 8192], P('vol', 'path'), may hold values from 0.5 to 4
- decisions: int32 [3, 64, 8192], P(None, 'vol', 'path'), may hold values 0 or 1
- level_range: int32 [4, 2], replicated, may hold values from 1 to 63, as said below
- w_in_master: float32 [64, 16, 1024], P('vol'), may hold values from -1.5 to 1.5
- w_mid_master: float32 [64, 1024, 1024], P('vol', 'path'), may hold values from -0.1875 to 0.1875
- vec_master: float32 [64, 3, 1024], P('vol'), may hold values from -0.6 to 0.6
- w_in_copy: bfloat16 [64, 16, 1024], P('vol'), may hold values from -1.5 to 1.5
- w_mid_copy: bfloat16 [64, 1024, 1024], P('vol', 'path'), may hold values from -0.1875 to 0.1875
- mom_in: float32 [64, 16, 1024], P('vol'), may hold values from -0.6 to 0.6
- mom_mid: float32 [64, 1024, 1024], P('vol', 'path'), may hold values from -0.6 to 0.6
- mom_vec: float32 [64, 3, 1024], P('vol'), may hold values from -0.6 to 0.6
Outputs:
- level_value: float32 [64], P('vol')
- new_w_in: float32 [64, 16, 1024], P('vol')
- new_w_mid: float32 [64, 1024, 1024], P('vol', 'path')
- new_vec: float32 [64, 3, 1024], P('vol')
- new_mom_in: float32 [64, 16, 1024], P('vol')
- new_mom_mid: float32 [64, 1024, 1024], P('vol', 'path')
- new_mom_vec: float32 [64, 3, 1024], P('vol')
- new_in_copy: bfloat16 [64, 16, 1024], P('vol')
- new_mid_copy: bfloat16 [64, 1024, 1024], P('vol', 'path')
The draws below stay inside these ranges and needn't reach their ends.
Inputs may be any that keep to these rules, and one draw needn't show every extreme that they name: At every date level_range[s, 0] <= level_range[s, 1] and level 0 lies below the range; at dates 1 to 3 the range starts at level 1; at date 0 the range holds exactly 32 levels.
All inputs are finite; a program needn't handle non-finite values. No bound on the sum of `decisions` on one device may be relied on, other than what follows from the above.
Results may differ from the reference program's by a relative error of at most 0.015.
Values may be sent and summed in bfloat16 or wider, within the bound.
A program may use at most 64 MiB of HBM per device.

```python
import math
import jax
import jax.numpy as jnp
from jax import lax

FACTORS = 16
HIDDEN_SIZE = 1024
DATES = 4
LEVELS = 64
PATHS = 8192


def draw_level_range(key, part):
    key_upper, key_start = jax.random.split(key, 2)
    lower_end = jnp.ones((DATES,), jnp.int32)
    upper_end = jax.random.randint(key_upper, (DATES,), LEVELS // 2, LEVELS)
    start_low = jax.random.randint(key_start, (), 1, LEVELS // 2 + 1)
    lower_end = lower_end.at[0].set(start_low)
    upper_end = upper_end.at[0].set(start_low + LEVELS // 2 - 1)
    return jnp.stack([lower_end, upper_end], axis=1).astype(jnp.int32)


def place_ends(entries, key, least, high):
    dims = entries.shape
    place = [jax.random.randint(jax.random.fold_in(key, axis), (), 0, dims[axis]) for axis in range(len(dims))]
    entries = entries.at[tuple(place)].set(least)
    longest = dims.index(max(dims))
    place[longest] = (place[longest] + 1) % dims[longest]
    return entries.at[tuple(place)].set(high)


def block_levels(rng, dims, cuts, least, high):
    def one(position, blocks):
        heights = jax.random.uniform(jax.random.fold_in(jax.random.fold_in(rng, 6), position), (blocks,), jnp.float32, least / len(cuts), high / len(cuts))
        return jnp.repeat(jnp.exp(heights), dims[position] // blocks).reshape((-1,) + (1,) * (len(dims) - position - 1))

    factor_of = one(*cuts[0])
    for cut in cuts[1:]:
        factor_of = factor_of * one(*cut)
    return factor_of


def noise(own_key, shape, scale, limit, shards=(), kind=jnp.bfloat16):
    values = jax.random.normal(own_key, shape, jnp.float32) * scale
    if len(shards) > 0:
        values = block_levels(own_key, shape, shards, -0.22, 0.18) * values
    return jnp.clip(values, min=-limit, max=limit).astype(kind)


def setup_inputs(seed: int = 0) -> dict:
    seeds = jax.random.split(jax.random.key(seed), 14)
    factors = noise(seeds[0], (FACTORS, PATHS), 1.0, 6.0, ((1, 8),))
    payoff = noise(seeds[1], (DATES, PATHS), 1.0, 6.0, ((1, 8),), jnp.float32)
    terminal = jnp.clip(jnp.exp(math.log(4.0) - 2.0794415 * jax.random.uniform(seeds[2], (LEVELS, PATHS), jnp.float32) ** block_levels(seeds[2], (LEVELS, PATHS), ((0, 64), (1, 8)), -0.2, 0.2)), 0.5, 4.0)
    decisions = place_ends((jax.random.randint(seeds[3], (DATES - 1, LEVELS, PATHS), 0, 2) < 1).astype(jnp.int32), jax.random.fold_in(seeds[3], 1), 0, 1)
    level_range = draw_level_range(jax.random.fold_in(seeds[13], 71), 0)
    w_in_master = noise(seeds[5], (LEVELS, FACTORS, HIDDEN_SIZE), FACTORS ** -0.5, 1.5, ((0, 64),), jnp.float32)
    w_mid_master = noise(seeds[6], (LEVELS, HIDDEN_SIZE, HIDDEN_SIZE), HIDDEN_SIZE ** -0.5, 0.1875, ((0, 64), (1, 8)), jnp.float32)
    vec_master = noise(seeds[7], (LEVELS, 3, HIDDEN_SIZE), 0.1, 0.6, ((0, 64),), jnp.float32)
    w_in_copy = noise(seeds[8], (LEVELS, FACTORS, HIDDEN_SIZE), FACTORS ** -0.5, 1.5, ((0, 64),))
    w_mid_copy = noise(seeds[9], (LEVELS, HIDDEN_SIZE, HIDDEN_SIZE), HIDDEN_SIZE ** -0.5, 0.1875, ((0, 64), (1, 8)))
    mom_in = noise(seeds[10], (LEVELS, FACTORS, HIDDEN_SIZE), 0.1, 0.6, ((0, 64),), jnp.float32)
    mom_mid = noise(seeds[11], (LEVELS, HIDDEN_SIZE, HIDDEN_SIZE), 0.1, 0.6, ((0, 64), (1, 8)), jnp.float32)
    mom_vec = noise(seeds[12], (LEVELS, 3, HIDDEN_SIZE), 0.1, 0.6, ((0, 64),), jnp.float32)
    return {"factors": factors, "payoff": payoff, "terminal": terminal, "decisions": decisions, "level_range": level_range, "w_in_master": w_in_master, "w_mid_master": w_mid_master, "vec_master": vec_master, "w_in_copy": w_in_copy, "w_mid_copy": w_mid_copy, "mom_in": mom_in, "mom_mid": mom_mid, "mom_vec": mom_vec}


MOMENTUM = 0.9
STEP_SIZE = 0.01


def silu_parts(preact):
    squash = jax.nn.sigmoid(preact)
    return preact * squash, squash * (1.0 + preact * (1.0 - squash))


def level_pass(w_first, w_second, vectors, features, gain_row):
    pre_one = lax.dot_general(features, w_first, (((0,), (0,)), ((), ())), preferred_element_type=jnp.float32) + vectors[0]
    act_one, slope_one = silu_parts(pre_one)
    hidden_one = act_one.astype(jnp.bfloat16)
    pre_two = jnp.dot(hidden_one, w_second, preferred_element_type=jnp.float32) + vectors[1]
    act_two, slope_two = silu_parts(pre_two)
    hidden_two = act_two.astype(jnp.bfloat16)
    logits = jnp.sum(hidden_two.astype(jnp.float32) * vectors[2], axis=1)
    chance = jax.nn.sigmoid(logits)
    d_logit = -gain_row * chance * (1.0 - chance)
    d_head = jnp.sum(d_logit[:, None] * hidden_two.astype(jnp.float32), axis=0)
    d_pre_two = d_logit[:, None] * vectors[2] * slope_two
    d_bias_two = jnp.sum(d_pre_two, axis=0)
    d_two_low = d_pre_two.astype(jnp.bfloat16)
    d_second = lax.dot_general(hidden_one, d_two_low, (((0,), (0,)), ((), ())), preferred_element_type=jnp.float32)
    d_hidden_one = lax.dot_general(d_two_low, w_second, (((1,), (1,)), ((), ())), preferred_element_type=jnp.float32)
    d_pre_one = d_hidden_one * slope_one
    d_bias_one = jnp.sum(d_pre_one, axis=0)
    d_first = jnp.dot(features, d_pre_one.astype(jnp.bfloat16), preferred_element_type=jnp.float32)
    d_vectors = jnp.stack([d_bias_one, d_bias_two, d_head])
    return d_first, d_second, d_vectors, jnp.sum(chance * gain_row)


def reference(factors, payoff, terminal, decisions, level_range, w_in_master, w_mid_master, vec_master, w_in_copy, w_mid_copy, mom_in, mom_mid, mom_vec):
    levels = jnp.arange(LEVELS, dtype=jnp.int32)[:, None]
    zero_row = jnp.zeros((1, PATHS), jnp.float32)
    carry_value = terminal
    for date_index in range(DATES - 1, 0, -1):
        lower_row = jnp.concatenate([zero_row, carry_value[:-1]], axis=0)
        lower_end = level_range[date_index, 0]
        upper_end = level_range[date_index, 1]
        inside = jnp.logical_and(levels >= lower_end, levels <= upper_end)
        taken_now = jnp.where(levels > upper_end, 1.0, jnp.where(inside, decisions[date_index - 1].astype(jnp.float32), 0.0))
        carry_value = taken_now * (payoff[date_index] + lower_row) + (1.0 - taken_now) * carry_value
    lower_row = jnp.concatenate([zero_row, carry_value[:-1]], axis=0)
    gain_all = payoff[0] + lower_row - carry_value
    low_now = level_range[0, 0]
    high_now = level_range[0, 1]
    active_span = LEVELS // 2

    def select_active(array):
        return lax.dynamic_slice_in_dim(array, low_now, active_span, 0)

    def one_level(level_items):
        return level_pass(level_items[0], level_items[1], level_items[2], factors, level_items[3])

    d_first, d_second, d_vectors, value_sums = lax.map(one_level, (select_active(w_in_copy), select_active(w_mid_copy), select_active(vec_master), select_active(gain_all)))

    def put_back(block, shape):
        return lax.dynamic_update_slice_in_dim(jnp.zeros(shape, jnp.float32), block, low_now, 0)

    grad_in = put_back(d_first, w_in_master.shape)
    grad_mid = put_back(d_second, w_mid_master.shape)
    grad_vec = put_back(d_vectors, vec_master.shape)
    value_active = put_back(value_sums, (LEVELS,))
    level_ids = levels[:, 0]
    active = jnp.logical_and(level_ids >= low_now, level_ids <= high_now)
    forced = jnp.where(level_ids > high_now, 1.0, 0.0)
    value_total = jnp.where(active, value_active, forced * jnp.sum(gain_all, axis=1)) + jnp.sum(carry_value, axis=1)
    level_value = value_total / PATHS
    new_mom_in = MOMENTUM * mom_in + grad_in
    new_mom_mid = MOMENTUM * mom_mid + grad_mid
    new_mom_vec = MOMENTUM * mom_vec + grad_vec
    new_w_in = w_in_master - STEP_SIZE * new_mom_in
    new_w_mid = w_mid_master - STEP_SIZE * new_mom_mid
    new_vec = vec_master - STEP_SIZE * new_mom_vec
    return (level_value, new_w_in, new_w_mid, new_vec, new_mom_in, new_mom_mid, new_mom_vec, new_w_in.astype(jnp.bfloat16), new_w_mid.astype(jnp.bfloat16))
```

```python
import jax
import jax.numpy as jnp
from jax import lax
from jax.experimental import pallas as pl
from jax.experimental.pallas import tpu as pltpu
from jax.sharding import PartitionSpec as P

MOMENTUM = 0.9
STEP_SIZE = 0.01
CHIPS = 4
HALVES = 2
F32 = jnp.float32
BF16 = jnp.bfloat16
ORDER = ((3, 2, 1, 0), (3, 0, 2, 1), (0, 3, 1, 2), (0, 1, 2, 3))


def from_behind(value, axis, steps):
    count = lax.axis_size(axis)
    return lax.ppermute(value, axis, [(source, source + steps) for source in range(count - steps)])


def sigmoid(u):
    return 0.5 * jnp.tanh(0.5 * u) + 0.5


def step_kernel(
    fac_ref,
    win_ref,
    vec_ref,
    shard_ref,
    gain_ref,
    rest_ref,
    mid_ref,
    small_ref,
    wfull,
    h1,
    h1t,
    slope,
    pre2,
    d2,
    grads,
    to_pair,
    from_pair,
    to_line,
    from_line,
    gain_col,
    small,
    small_pair,
    small_chip,
    small_sum,
    ag_send,
    ag_recv,
    pair_send,
    pair_recv,
    line_send,
    line_recv,
    small_send,
    small_recv,
    chip_send,
    chip_recv,
    sum_send,
    sum_recv,
):
    me = lax.axis_index("path")
    c = me // 2
    k = me % 2
    other = me + 1 - 2 * k
    hidden = h1.shape[1]
    paths = h1.shape[0]
    depth = shard_ref.shape[0]
    part = depth // HALVES
    half_columns = hidden // 2

    def remote(src, dst, send, recv, to):
        return pltpu.make_async_remote_copy(
            src_ref=src,
            dst_ref=dst,
            send_sem=send,
            recv_sem=recv,
            device_id={"path": to},
            device_id_type=pl.DeviceIdType.MESH,
        )

    barrier = pltpu.get_barrier_semaphore()
    pl.semaphore_signal(barrier, inc=1, device_id={"path": other}, device_id_type=pl.DeviceIdType.MESH)
    for far in range(1, CHIPS):
        pl.semaphore_signal(
            barrier,
            inc=1,
            device_id={"path": ((c + far) % CHIPS) * 2 + k},
            device_id_type=pl.DeviceIdType.MESH,
        )

    rows_first = 128
    gain_col[...] = jnp.transpose(jnp.broadcast_to(gain_ref[...], (8, paths)))

    def first_layer(m, carry):
        at = pl.ds(pl.multiple_of(m * rows_first, rows_first), rows_first)
        pre = (
            lax.dot_general(
                fac_ref[:, at], win_ref[...], (((0,), (0,)), ((), ())), preferred_element_type=F32
            )
            + vec_ref[0:1, :]
        )
        s = sigmoid(pre)
        act = pre * s
        slope[at, :] = s * (1.0 + pre * (1.0 - s))
        h1[at, :] = act.astype(BF16)
        h1t[:, at] = jnp.transpose(act).astype(BF16)
        return carry

    tiles_first = paths // rows_first
    lax.fori_loop(0, 1, first_layer, 0)
    pl.semaphore_wait(barrier, CHIPS)

    def rows_of(slot, h):
        return pl.ds(pl.multiple_of(slot * depth + h * part, part), part)

    LEFT, RIGHT, PAIR = 0, 1, 2

    def gather_copy(source, slot, h, way, to):
        return remote(
            source, wfull.at[rows_of(slot, h), :], ag_send.at[way, slot, h], ag_recv.at[slot, h], to
        )

    def shard_part(h):
        return shard_ref.at[pl.ds(h * part, part), :]

    for h in range(HALVES):

        @pl.when(c > 0)
        def _():
            gather_copy(shard_part(h), me, h, LEFT, me - 2).start()

        @pl.when(c < CHIPS - 1)
        def _():
            gather_copy(shard_part(h), me, h, RIGHT, me + 2).start()

    for h in range(HALVES):
        gather_copy(shard_part(h), me, h, PAIR, other).start()
    wfull[pl.ds(pl.multiple_of(me * depth, depth), depth), :] = shard_ref[...]
    lax.fori_loop(1, tiles_first, first_layer, 0)

    def landed(slot, h):
        at = wfull.at[rows_of(slot, h), :]
        gather_copy(at, slot, h, PAIR, other).wait_recv()

    def forward(slot, h, way, to):
        gather_copy(wfull.at[rows_of(slot, h), :], slot, h, way, to).start()

    def relay(far):
        for h in range(HALVES):

            @pl.when(c >= far)
            def _():
                slot = me - 2 * far
                landed(slot, h)

                @pl.when(c < CHIPS - 1)
                def _():
                    forward(slot, h, RIGHT, me + 2)

                forward(slot, h, PAIR, other)

            @pl.when(c + far < CHIPS)
            def _():
                slot = me + 2 * far
                landed(slot, h)

                @pl.when(c > 0)
                def _():
                    forward(slot, h, LEFT, me - 2)

                forward(slot, h, PAIR, other)

    tile = 256

    def middle(chip, first):
        columns = pl.ds(pl.multiple_of(chip * 2 * depth, 2 * depth), 2 * depth)

        def body(m, carry):
            at = pl.ds(pl.multiple_of(m * tile, tile), tile)
            product = jnp.dot(h1[at, columns], wfull[columns, :], preferred_element_type=F32)
            if first:
                pre2[at, :] = product + vec_ref[1:2, :]
            else:
                pre2[at, :] += product
            return carry

        lax.fori_loop(0, paths // tile, body, 0)

    def absorb(far):
        @pl.when(c >= far)
        def _():
            for h in range(HALVES):
                landed(other - 2 * far, h)
            middle(c - far, False)

        @pl.when(c + far < CHIPS)
        def _():
            for h in range(HALVES):
                landed(other + 2 * far, h)
            middle(c + far, False)

    relay(1)
    for h in range(HALVES):
        landed(other, h)
    middle(c, True)
    absorb(1)
    relay(2)
    absorb(2)
    relay(3)
    absorb(3)

    rows_second = 128

    def second_layer(m, carry):
        bias_two, head, value = carry
        at = pl.ds(pl.multiple_of(m * rows_second, rows_second), rows_second)
        pre = pre2[at, :]
        s = sigmoid(pre)
        act = (pre * s).astype(BF16).astype(F32)
        weights = vec_ref[2:3, :]
        chance = sigmoid(jnp.sum(act * weights, axis=1, keepdims=True))
        gain = gain_col[at, 0:1]
        d_logit = -gain * chance * (1.0 - chance)
        d_pre = d_logit * weights * (s * (1.0 + pre * (1.0 - s)))
        d2[at, :] = d_pre.astype(BF16)
        bias_two = bias_two + jnp.sum(d_pre, axis=0, keepdims=True)
        head = head + jnp.sum(d_logit * act, axis=0, keepdims=True)
        value = value + jnp.sum(chance * gain, axis=0, keepdims=True)
        return bias_two, head, value

    zero_row = jnp.zeros((1, hidden), F32)
    bias_two, head, value = lax.fori_loop(
        0, paths // rows_second, second_layer, (zero_row, zero_row, jnp.zeros((1, 1), F32))
    )
    small[17:18, :] = bias_two
    small[18:19, :] = head
    lane = lax.broadcasted_iota(jnp.int32, (1, hidden), 1)
    small[19:20, :] = rest_ref[...] + jnp.where(lane == 0, value, 0.0)
    small[20:24, :] = jnp.zeros((4, hidden), F32)

    def order(step):
        packed = sum(ORDER[chip][step] * 4**chip for chip in range(CHIPS))
        return lax.rem(lax.shift_right_logical(jnp.int32(packed), 2 * c), jnp.int32(4))

    def pair_copy(e):
        return remote(to_pair.at[e], from_pair.at[e], pair_send.at[e], pair_recv.at[e], other)

    def product(step):
        e = order(step)
        rows = pl.ds(pl.multiple_of(e * 2 * depth, 2 * depth), 2 * depth)

        def body(n, carry):
            at = pl.ds(pl.multiple_of(n * tile, tile), tile)
            grads[e, :, at] = jnp.dot(h1t[rows, :], d2[:, at], preferred_element_type=F32)
            return carry

        lax.fori_loop(0, hidden // tile, body, 0)
        theirs = pl.ds(pl.multiple_of((1 - k) * depth, depth), depth)
        to_pair[e] = grads[e, theirs, :].astype(BF16)
        pair_copy(e).start()

    def line_copy(way, e, h, to):
        at = pl.ds(h * part, part)
        return remote(
            to_line.at[e, at, :],
            from_line.at[way, e, at, :],
            line_send.at[e, h],
            line_recv.at[way, e, h],
            to,
        )

    def own_part(e, h):
        mine = pl.ds(pl.multiple_of(k * depth + h * part, part), part)
        return grads[e, mine, :] + from_pair[e, pl.ds(h * part, part), :].astype(F32)

    def along_line(step):
        e = order(step)
        pair_copy(e).wait_recv()
        for h in range(HALVES):
            at = pl.ds(h * part, part)

            @pl.when(e > c)
            def _():
                @pl.when(c == 0)
                def _():
                    to_line[e, at, :] = own_part(e, h).astype(BF16)

                @pl.when(c > 0)
                def _():
                    line_copy(0, e, h, other).wait_recv()
                    total = own_part(e, h) + from_line[0, e, at, :].astype(F32)
                    to_line[e, at, :] = total.astype(BF16)

                line_copy(0, e, h, me + 2).start()

            @pl.when(e < c)
            def _():
                @pl.when(c == CHIPS - 1)
                def _():
                    to_line[e, at, :] = own_part(e, h).astype(BF16)

                @pl.when(c < CHIPS - 1)
                def _():
                    line_copy(1, e, h, other).wait_recv()
                    total = own_part(e, h) + from_line[1, e, at, :].astype(F32)
                    to_line[e, at, :] = total.astype(BF16)

                line_copy(1, e, h, me - 2).start()

    at_end = c * (CHIPS - 1 - c) == 0
    product(0)
    product(1)
    pl.when(at_end)(lambda: along_line(0))
    product(2)
    pl.when(at_end)(lambda: along_line(1))
    product(3)
    pl.when(at_end)(lambda: along_line(2))

    def back(m, carry):
        bias_one, first = carry
        at = pl.ds(pl.multiple_of(m * tile, tile), tile)
        d_pre = (
            lax.dot_general(
                d2[at, :], wfull[...], (((1,), (1,)), ((), ())), preferred_element_type=F32
            )
            * slope[at, :]
        )
        bias_one = bias_one + jnp.sum(d_pre, axis=0, keepdims=True)
        first = first + jnp.dot(fac_ref[:, at], d_pre.astype(BF16), preferred_element_type=F32)
        return bias_one, first

    bias_one, first = lax.fori_loop(
        0, paths // tile, back, (zero_row, jnp.zeros((fac_ref.shape[0], hidden), F32))
    )
    small[0:16, :] = first
    small[16:17, :] = bias_one

    my_columns = pl.ds(pl.multiple_of(k * half_columns, half_columns), half_columns)
    their_columns = pl.ds(pl.multiple_of((1 - k) * half_columns, half_columns), half_columns)
    pair_sum = remote(small, small_pair, small_send, small_recv, other)
    pair_sum.start()
    pl.when(jnp.logical_not(at_end))(lambda: along_line(0))
    pair_sum.wait_recv()
    small_chip[c] = small[:, my_columns] + small_pair[:, my_columns]

    def chip_copy(far):
        to = ((c + far) % CHIPS) * 2 + k
        return remote(
            small_chip.at[c], small_chip.at[c], chip_send.at[far - 1], chip_recv.at[c], to
        )

    def chip_landed(far):
        chip = (c + far) % CHIPS
        slot = small_chip.at[chip]
        remote(slot, slot, chip_send.at[far - 1], chip_recv.at[chip], other).wait_recv()

    for far in range(1, CHIPS):
        chip_copy(far).start()
    pl.when(jnp.logical_not(at_end))(lambda: along_line(1))
    pl.when(jnp.logical_not(at_end))(lambda: along_line(2))
    for far in range(1, CHIPS):
        chip_landed(far)
    small_sum[:, my_columns] = small_chip[0] + small_chip[1] + small_chip[2] + small_chip[3]
    mine = small_sum.at[:, my_columns]
    theirs = small_sum.at[:, their_columns]
    share = remote(mine, mine, sum_send, sum_recv, other)
    share.start()

    pair_copy(c).wait_recv()
    for h in range(HALVES):
        mid_ref[pl.ds(h * part, part), :] = own_part(c, h)

    def arrived(way):
        for h in range(HALVES):
            at = pl.ds(h * part, part)
            line_copy(way, c, h, other).wait_recv()
            mid_ref[at, :] += from_line[way, c, at, :].astype(F32)

    pl.when(c > 0)(lambda: arrived(0))
    pl.when(c < CHIPS - 1)(lambda: arrived(1))
    remote(theirs, theirs, sum_send, sum_recv, other).wait_recv()
    small_ref[...] = small_sum[...]

    for h in range(HALVES):
        gather_copy(shard_part(h), me, h, PAIR, other).wait_send()

        @pl.when(c > 0)
        def _():
            gather_copy(shard_part(h), me, h, LEFT, me - 2).wait_send()

        @pl.when(c < CHIPS - 1)
        def _():
            gather_copy(shard_part(h), me, h, RIGHT, me + 2).wait_send()

        for far in range(1, CHIPS):

            @pl.when(c >= far)
            def _():
                slot = me - 2 * far
                source = wfull.at[rows_of(slot, h), :]
                gather_copy(source, slot, h, PAIR, other).wait_send()

                @pl.when(c < CHIPS - 1)
                def _():
                    gather_copy(source, slot, h, RIGHT, me + 2).wait_send()

            @pl.when(c + far < CHIPS)
            def _():
                slot = me + 2 * far
                source = wfull.at[rows_of(slot, h), :]
                gather_copy(source, slot, h, PAIR, other).wait_send()

                @pl.when(c > 0)
                def _():
                    gather_copy(source, slot, h, LEFT, me - 2).wait_send()

    for e in range(CHIPS):
        pair_copy(e).wait_send()
    for step in range(CHIPS - 1):
        for h in range(HALVES):
            line_copy(0, order(step), h, other).wait_send()
    pair_sum.wait_send()
    for far in range(1, CHIPS):
        chip_copy(far).wait_send()
    share.wait_send()


def run_step(factors, w_first, vectors, shard, gain_row, rest_row):
    paths = factors.shape[1]
    depth, hidden = shard.shape
    part_count = HALVES
    dma = pltpu.SemaphoreType.DMA
    vmem = pl.BlockSpec(memory_space=pltpu.VMEM)
    return pl.pallas_call(
        step_kernel,
        out_shape=(
            jax.ShapeDtypeStruct((depth, hidden), F32),
            jax.ShapeDtypeStruct((24, hidden), F32),
        ),
        in_specs=[vmem] * 6,
        out_specs=(vmem, vmem),
        scratch_shapes=[
            pltpu.VMEM((hidden, hidden), BF16),
            pltpu.VMEM((paths, hidden), BF16),
            pltpu.VMEM((hidden, paths), BF16),
            pltpu.VMEM((paths, hidden), F32),
            pltpu.VMEM((paths, hidden), F32),
            pltpu.VMEM((paths, hidden), BF16),
            pltpu.VMEM((CHIPS, 2 * depth, hidden), F32),
            pltpu.VMEM((CHIPS, depth, hidden), BF16),
            pltpu.VMEM((CHIPS, depth, hidden), BF16),
            pltpu.VMEM((CHIPS, depth, hidden), BF16),
            pltpu.VMEM((2, CHIPS, depth, hidden), BF16),
            pltpu.VMEM((paths, 8), F32),
            pltpu.VMEM((24, hidden), F32),
            pltpu.VMEM((24, hidden), F32),
            pltpu.VMEM((CHIPS, 24, hidden // 2), F32),
            pltpu.VMEM((24, hidden), F32),
            dma((3, 2 * CHIPS, part_count)),
            dma((2 * CHIPS, part_count)),
            dma((CHIPS,)),
            dma((CHIPS,)),
            dma((CHIPS, part_count)),
            dma((2, CHIPS, part_count)),
            dma,
            dma,
            dma((CHIPS - 1,)),
            dma((CHIPS,)),
            dma,
            dma,
        ],
        compiler_params=pltpu.CompilerParams(collective_id=0, has_side_effects=True),
        cost_estimate=pl.CostEstimate(
            flops=6 * paths * hidden * hidden, bytes_accessed=4 * hidden * hidden, transcendentals=0
        ),
    )(factors, w_first, vectors, shard, gain_row, rest_row)


def shards(
    factors,
    payoff,
    terminal,
    decisions,
    level_range,
    w_in_master,
    w_mid_master,
    vec_master,
    w_in_copy,
    w_mid_copy,
    mom_in,
    mom_mid,
    mom_vec,
):
    level_here = lax.axis_index("vol")
    dates = payoff.shape[0]
    paths_total = payoff.shape[1] * lax.axis_size("path")
    packed = jnp.concatenate([terminal, decisions[:, 0].astype(F32)], axis=0)
    below = [packed] + [from_behind(packed, "vol", back) for back in range(1, dates + 1)]
    carry = [rows[0] for rows in below]
    for date_index in range(dates - 1, 0, -1):
        lower_end = level_range[date_index, 0]
        upper_end = level_range[date_index, 1]
        after = []
        for j in range(len(carry) - 1):
            level = level_here - j
            inside = jnp.logical_and(level >= lower_end, level <= upper_end)
            taken = jnp.where(level > upper_end, 1.0, jnp.where(inside, below[j][date_index], 0.0))
            after.append(taken * (payoff[date_index] + carry[j + 1]) + (1.0 - taken) * carry[j])
        carry = after
    gain_row = payoff[0] + carry[1] - carry[0]
    low_now = level_range[0, 0]
    high_now = level_range[0, 1]
    active = jnp.logical_and(level_here >= low_now, level_here <= high_now)
    rest_row = jnp.where(level_here > high_now, gain_row, 0.0) + carry[0]
    gain_active = jnp.where(active, gain_row, 0.0)
    mid_grad, small = run_step(
        factors, w_in_copy[0], vec_master[0], w_mid_copy[0], gain_active[None], rest_row[None]
    )
    level_value = (jnp.sum(small[19]) / paths_total)[None]
    new_mom_in = MOMENTUM * mom_in + small[None, 0:16]
    new_mom_mid = MOMENTUM * mom_mid + mid_grad[None]
    new_mom_vec = MOMENTUM * mom_vec + small[None, 16:19]
    new_w_in = w_in_master - STEP_SIZE * new_mom_in
    new_w_mid = w_mid_master - STEP_SIZE * new_mom_mid
    new_vec = vec_master - STEP_SIZE * new_mom_vec
    return (
        level_value,
        new_w_in,
        new_w_mid,
        new_vec,
        new_mom_in,
        new_mom_mid,
        new_mom_vec,
        new_w_in.astype(BF16),
        new_w_mid.astype(BF16),
    )


def solution(mesh):
    in_specs = (
        P(None, "path"),
        P(None, "path"),
        P("vol", "path"),
        P(None, "vol", "path"),
        P(),
        P("vol", None, None),
        P("vol", "path", None),
        P("vol", None, None),
        P("vol", None, None),
        P("vol", "path", None),
        P("vol", None, None),
        P("vol", "path", None),
        P("vol", None, None),
    )
    out_specs = (
        P("vol"),
        P("vol", None, None),
        P("vol", "path", None),
        P("vol", None, None),
        P("vol", None, None),
        P("vol", "path", None),
        P("vol", None, None),
        P("vol", None, None),
        P("vol", "path", None),
    )
    return jax.shard_map(shards, mesh=mesh, in_specs=in_specs, out_specs=out_specs, check_vma=False)
```

```python
import functools

import jax
import jax.numpy as jnp
from jax import lax
from jax.experimental import pallas as pl
from jax.experimental.pallas import tpu as pltpu
from jax.sharding import PartitionSpec as P

MOMENTUM = 0.9
STEP_SIZE = 0.01
CHIPS = 4
HALVES = 2
F32 = jnp.float32
BF16 = jnp.bfloat16
ORDER = ((3, 2, 1, 0), (3, 0, 2, 1), (0, 3, 1, 2), (0, 1, 2, 3))


def sigmoid(u):
    return 0.5 * jnp.tanh(0.5 * u) + 0.5


def step_kernel(
    range_ref,
    fac_ref,
    payoff_ref,
    terminal_ref,
    decisions_ref,
    win_ref,
    vec_ref,
    shard_ref,
    mid_ref,
    small_ref,
    wfull,
    h1,
    h1t,
    slope,
    pre2,
    d2,
    grads,
    to_pair,
    from_pair,
    to_line,
    from_line,
    level_out,
    level_in,
    gain_col,
    small,
    small_pair,
    small_chip,
    small_sum,
    level_send,
    level_recv,
    ag_send,
    ag_recv,
    pair_send,
    pair_recv,
    line_send,
    line_recv,
    small_send,
    small_recv,
    chip_send,
    chip_recv,
    sum_send,
    sum_recv,
):
    level = lax.axis_index("vol")
    levels = lax.axis_size("vol")
    dates = payoff_ref.shape[0]
    me = lax.axis_index("path")
    c = me // 2
    k = me % 2
    other = me + 1 - 2 * k
    hidden = h1.shape[1]
    paths = h1.shape[0]
    depth = shard_ref.shape[1]
    part = depth // HALVES
    half_columns = hidden // 2

    def remote(src, dst, send, recv, to):
        return pltpu.make_async_remote_copy(
            src_ref=src,
            dst_ref=dst,
            send_sem=send,
            recv_sem=recv,
            device_id={"path": to},
            device_id_type=pl.DeviceIdType.MESH,
        )

    barrier = pltpu.get_barrier_semaphore()
    for back in range(1, dates + 1):
        for level_to in ((level + back) % levels, (level + levels - back) % levels):
            pl.semaphore_signal(
                barrier, inc=1, device_id={"vol": level_to}, device_id_type=pl.DeviceIdType.MESH
            )
    pl.semaphore_signal(barrier, inc=1, device_id={"path": other}, device_id_type=pl.DeviceIdType.MESH)
    for far in range(1, CHIPS):
        pl.semaphore_signal(
            barrier,
            inc=1,
            device_id={"path": ((c + far) % CHIPS) * 2 + k},
            device_id_type=pl.DeviceIdType.MESH,
        )

    level_out[0:1, :] = terminal_ref[...]
    for date in range(1, dates):
        level_out[date : date + 1, :] = decisions_ref[date - 1].astype(F32)

    def level_copy(back):
        return pltpu.make_async_remote_copy(
            src_ref=level_out,
            dst_ref=level_in.at[back - 1],
            send_sem=level_send.at[back - 1],
            recv_sem=level_recv.at[back - 1],
            device_id={"vol": (level + back) % levels},
            device_id_type=pl.DeviceIdType.MESH,
        )

    rows_first = 128

    def first_layer(m, carry):
        at = pl.ds(pl.multiple_of(m * rows_first, rows_first), rows_first)
        pre = (
            lax.dot_general(
                fac_ref[:, at], win_ref[0], (((0,), (0,)), ((), ())), preferred_element_type=F32
            )
            + vec_ref[0]
        )
        s = sigmoid(pre)
        act = pre * s
        slope[at, :] = s * (1.0 + pre * (1.0 - s))
        h1[at, :] = act.astype(BF16)
        h1t[:, at] = jnp.transpose(act).astype(BF16)
        return carry

    tiles_first = paths // rows_first
    tiles_ahead = tiles_first // 2
    lax.fori_loop(0, tiles_ahead, first_layer, 0)
    pl.semaphore_wait(barrier, CHIPS + 2 * dates)

    def rows_of(slot, h):
        return pl.ds(pl.multiple_of(slot * depth + h * part, part), part)

    LEFT, RIGHT, PAIR = 0, 1, 2

    def gather_copy(source, slot, h, way, to):
        return remote(
            source, wfull.at[rows_of(slot, h), :], ag_send.at[way, slot, h], ag_recv.at[slot, h], to
        )

    def shard_part(h):
        return shard_ref.at[0, pl.ds(h * part, part), :]

    for h in range(HALVES):

        @pl.when(c > 0)
        def _():
            gather_copy(shard_part(h), me, h, LEFT, me - 2).start()

        @pl.when(c < CHIPS - 1)
        def _():
            gather_copy(shard_part(h), me, h, RIGHT, me + 2).start()

    for h in range(HALVES):
        gather_copy(shard_part(h), me, h, PAIR, other).start()
    wfull[pl.ds(pl.multiple_of(me * depth, depth), depth), :] = shard_ref[0]
    for back in range(1, dates + 1):
        level_copy(back).start()
    lax.fori_loop(tiles_ahead, tiles_first, first_layer, 0)

    def landed(slot, h):
        at = wfull.at[rows_of(slot, h), :]
        gather_copy(at, slot, h, PAIR, other).wait_recv()

    def forward(slot, h, way, to):
        gather_copy(wfull.at[rows_of(slot, h), :], slot, h, way, to).start()

    def relay(far):
        for h in range(HALVES):

            @pl.when(c >= far)
            def _():
                slot = me - 2 * far
                landed(slot, h)

                @pl.when(c < CHIPS - 1)
                def _():
                    forward(slot, h, RIGHT, me + 2)

                forward(slot, h, PAIR, other)

            @pl.when(c + far < CHIPS)
            def _():
                slot = me + 2 * far
                landed(slot, h)

                @pl.when(c > 0)
                def _():
                    forward(slot, h, LEFT, me - 2)

                forward(slot, h, PAIR, other)

    tile = 256

    def middle(chip, first):
        columns = pl.ds(pl.multiple_of(chip * 2 * depth, 2 * depth), 2 * depth)

        def body(m, carry):
            at = pl.ds(pl.multiple_of(m * tile, tile), tile)
            product = jnp.dot(h1[at, columns], wfull[columns, :], preferred_element_type=F32)
            if first:
                pre2[at, :] = product + vec_ref[1]
            else:
                pre2[at, :] += product
            return carry

        lax.fori_loop(0, paths // tile, body, 0)

    def absorb(far):
        @pl.when(c >= far)
        def _():
            for h in range(HALVES):
                landed(other - 2 * far, h)
            middle(c - far, False)

        @pl.when(c + far < CHIPS)
        def _():
            for h in range(HALVES):
                landed(other + 2 * far, h)
            middle(c + far, False)

    relay(1)
    for h in range(HALVES):
        landed(other, h)
    middle(c, True)
    absorb(1)
    relay(2)

    for back in range(1, dates + 1):
        level_copy(back).wait_recv()

    def of_level(back, row):
        if back == 0:
            return level_out[row : row + 1, :]
        return jnp.where(level >= back, level_in[back - 1, row : row + 1, :], 0.0)

    carry = [of_level(back, 0) for back in range(dates + 1)]
    for date in range(dates - 1, 0, -1):
        lower_end, upper_end = range_ref[0, date], range_ref[1, date]
        after = []
        for back in range(len(carry) - 1):
            here = level - back
            inside = jnp.logical_and(here >= lower_end, here <= upper_end)
            free = jnp.where(inside, of_level(back, date), 0.0)
            taken = jnp.where(here > upper_end, 1.0, free)
            paid = payoff_ref[date : date + 1, :] + carry[back + 1]
            after.append(taken * paid + (1.0 - taken) * carry[back])
        carry = after
    gain_row = payoff_ref[0:1, :] + carry[1] - carry[0]
    active = jnp.logical_and(level >= range_ref[0, 0], level <= range_ref[1, 0])
    rest_row = jnp.where(level > range_ref[1, 0], gain_row, 0.0) + carry[0]
    gain_active = jnp.where(active, gain_row, 0.0)
    gain_col[...] = jnp.transpose(jnp.broadcast_to(gain_active, (8, paths)))
    small[19:20, :] = rest_row
    absorb(2)
    relay(3)
    absorb(3)

    rows_second = 128

    def second_layer(m, carry):
        bias_two, head, value = carry
        at = pl.ds(pl.multiple_of(m * rows_second, rows_second), rows_second)
        pre = pre2[at, :]
        s = sigmoid(pre)
        act = (pre * s).astype(BF16).astype(F32)
        weights = vec_ref[2]
        chance = sigmoid(jnp.sum(act * weights, axis=1, keepdims=True))
        gain = gain_col[at, 0:1]
        d_logit = -gain * chance * (1.0 - chance)
        d_pre = d_logit * weights * (s * (1.0 + pre * (1.0 - s)))
        d2[at, :] = d_pre.astype(BF16)
        bias_two = bias_two + jnp.sum(d_pre, axis=0, keepdims=True)
        head = head + jnp.sum(d_logit * act, axis=0, keepdims=True)
        value = value + jnp.sum(chance * gain, axis=0, keepdims=True)
        return bias_two, head, value

    zero_row = jnp.zeros((1, hidden), F32)
    bias_two, head, value = lax.fori_loop(
        0, paths // rows_second, second_layer, (zero_row, zero_row, jnp.zeros((1, 1), F32))
    )
    small[17:18, :] = bias_two
    small[18:19, :] = head
    lane = lax.broadcasted_iota(jnp.int32, (1, hidden), 1)
    small[19:20, :] += jnp.where(lane == 0, value, 0.0)
    small[20:24, :] = jnp.zeros((4, hidden), F32)

    def order(step):
        packed = sum(ORDER[chip][step] * 4**chip for chip in range(CHIPS))
        return lax.rem(lax.shift_right_logical(jnp.int32(packed), 2 * c), jnp.int32(4))

    def pair_copy(e):
        return remote(to_pair.at[e], from_pair.at[e], pair_send.at[e], pair_recv.at[e], other)

    def product(step):
        e = order(step)
        rows = pl.ds(pl.multiple_of(e * 2 * depth, 2 * depth), 2 * depth)

        def body(n, carry):
            at = pl.ds(pl.multiple_of(n * tile, tile), tile)
            grads[e, :, at] = jnp.dot(h1t[rows, :], d2[:, at], preferred_element_type=F32)
            return carry

        lax.fori_loop(0, hidden // tile, body, 0)
        theirs = pl.ds(pl.multiple_of((1 - k) * depth, depth), depth)
        to_pair[e] = grads[e, theirs, :].astype(BF16)
        pair_copy(e).start()

    def line_copy(way, e, h, to):
        at = pl.ds(h * part, part)
        return remote(
            to_line.at[e, at, :],
            from_line.at[way, e, at, :],
            line_send.at[e, h],
            line_recv.at[way, e, h],
            to,
        )

    def own_part(e, h):
        mine = pl.ds(pl.multiple_of(k * depth + h * part, part), part)
        return grads[e, mine, :] + from_pair[e, pl.ds(h * part, part), :].astype(F32)

    def along_line(step, halves=range(HALVES)):
        e = order(step)
        if 0 in halves:
            pair_copy(e).wait_recv()
        for h in halves:
            at = pl.ds(h * part, part)

            @pl.when(e > c)
            def _():
                @pl.when(c == 0)
                def _():
                    to_line[e, at, :] = own_part(e, h).astype(BF16)

                @pl.when(c > 0)
                def _():
                    line_copy(0, e, h, other).wait_recv()
                    total = own_part(e, h) + from_line[0, e, at, :].astype(F32)
                    to_line[e, at, :] = total.astype(BF16)

                line_copy(0, e, h, me + 2).start()

            @pl.when(e < c)
            def _():
                @pl.when(c == CHIPS - 1)
                def _():
                    to_line[e, at, :] = own_part(e, h).astype(BF16)

                @pl.when(c < CHIPS - 1)
                def _():
                    line_copy(1, e, h, other).wait_recv()
                    total = own_part(e, h) + from_line[1, e, at, :].astype(F32)
                    to_line[e, at, :] = total.astype(BF16)

                line_copy(1, e, h, me - 2).start()

    at_end = c * (CHIPS - 1 - c) == 0
    product(0)
    product(1)
    pl.when(at_end)(lambda: along_line(0))
    product(2)
    pl.when(at_end)(lambda: along_line(1))
    product(3)
    pl.when(at_end)(lambda: along_line(2))

    def back(m, carry):
        bias_one, first = carry
        at = pl.ds(pl.multiple_of(m * tile, tile), tile)
        d_pre = (
            lax.dot_general(
                d2[at, :], wfull[...], (((1,), (1,)), ((), ())), preferred_element_type=F32
            )
            * slope[at, :]
        )
        bias_one = bias_one + jnp.sum(d_pre, axis=0, keepdims=True)
        first = first + jnp.dot(fac_ref[:, at], d_pre.astype(BF16), preferred_element_type=F32)
        return bias_one, first

    def on_the_way(step, h):
        pl.when(jnp.logical_not(at_end))(lambda: along_line(step, (h,)))

    sums = (zero_row, jnp.zeros((fac_ref.shape[0], hidden), F32))
    sums = lax.fori_loop(0, paths // tile // 2, back, sums)
    on_the_way(0, 0)
    bias_one, first = lax.fori_loop(paths // tile // 2, paths // tile, back, sums)
    small[0:16, :] = first
    small[16:17, :] = bias_one

    my_columns = pl.ds(pl.multiple_of(k * half_columns, half_columns), half_columns)
    their_columns = pl.ds(pl.multiple_of((1 - k) * half_columns, half_columns), half_columns)
    pair_sum = remote(small, small_pair, small_send, small_recv, other)
    pair_sum.start()
    on_the_way(0, 1)
    pair_sum.wait_recv()
    small_chip[c] = small[:, my_columns] + small_pair[:, my_columns]

    def chip_copy(far):
        to = ((c + far) % CHIPS) * 2 + k
        return remote(
            small_chip.at[c], small_chip.at[c], chip_send.at[far - 1], chip_recv.at[c], to
        )

    def chip_landed(far):
        chip = (c + far) % CHIPS
        slot = small_chip.at[chip]
        remote(slot, slot, chip_send.at[far - 1], chip_recv.at[chip], other).wait_recv()

    for far in range(1, CHIPS):
        chip_copy(far).start()
    for h in range(HALVES):
        for step in (1, 2):
            on_the_way(step, h)
    for far in range(1, CHIPS):
        chip_landed(far)
    small_sum[:, my_columns] = small_chip[0] + small_chip[1] + small_chip[2] + small_chip[3]
    mine = small_sum.at[:, my_columns]
    theirs = small_sum.at[:, their_columns]
    share = remote(mine, mine, sum_send, sum_recv, other)
    share.start()

    pair_copy(c).wait_recv()
    for h in range(HALVES):
        mid_ref[pl.ds(h * part, part), :] = own_part(c, h)

    def arrived(way):
        for h in range(HALVES):
            at = pl.ds(h * part, part)
            line_copy(way, c, h, other).wait_recv()
            mid_ref[at, :] += from_line[way, c, at, :].astype(F32)

    pl.when(c > 0)(lambda: arrived(0))
    pl.when(c < CHIPS - 1)(lambda: arrived(1))
    remote(theirs, theirs, sum_send, sum_recv, other).wait_recv()
    small_ref[...] = small_sum[...]

    for back in range(1, dates + 1):
        level_copy(back).wait_send()
    for h in range(HALVES):
        gather_copy(shard_part(h), me, h, PAIR, other).wait_send()

        @pl.when(c > 0)
        def _():
            gather_copy(shard_part(h), me, h, LEFT, me - 2).wait_send()

        @pl.when(c < CHIPS - 1)
        def _():
            gather_copy(shard_part(h), me, h, RIGHT, me + 2).wait_send()

        for far in range(1, CHIPS):

            @pl.when(c >= far)
            def _():
                slot = me - 2 * far
                source = wfull.at[rows_of(slot, h), :]
                gather_copy(source, slot, h, PAIR, other).wait_send()

                @pl.when(c < CHIPS - 1)
                def _():
                    gather_copy(source, slot, h, RIGHT, me + 2).wait_send()

            @pl.when(c + far < CHIPS)
            def _():
                slot = me + 2 * far
                source = wfull.at[rows_of(slot, h), :]
                gather_copy(source, slot, h, PAIR, other).wait_send()

                @pl.when(c > 0)
                def _():
                    gather_copy(source, slot, h, LEFT, me - 2).wait_send()

    for e in range(CHIPS):
        pair_copy(e).wait_send()
    for step in range(CHIPS - 1):
        for h in range(HALVES):
            line_copy(0, order(step), h, other).wait_send()
    pair_sum.wait_send()
    for far in range(1, CHIPS):
        chip_copy(far).wait_send()
    share.wait_send()


def run_step(level_range, factors, payoff, terminal, decisions, w_first, vectors, shard):
    paths = factors.shape[1]
    dates = payoff.shape[0]
    _, depth, hidden = shard.shape
    part_count = HALVES
    dma = pltpu.SemaphoreType.DMA
    vmem = pl.BlockSpec(memory_space=pltpu.VMEM)
    return pl.pallas_call(
        step_kernel,
        out_shape=(
            jax.ShapeDtypeStruct((depth, hidden), F32),
            jax.ShapeDtypeStruct((24, hidden), F32),
        ),
        in_specs=[pl.BlockSpec(memory_space=pltpu.SMEM)] + [vmem] * 7,
        out_specs=(vmem, vmem),
        scratch_shapes=[
            pltpu.VMEM((hidden, hidden), BF16),
            pltpu.VMEM((paths, hidden), BF16),
            pltpu.VMEM((hidden, paths), BF16),
            pltpu.VMEM((paths, hidden), F32),
            pltpu.VMEM((paths, hidden), F32),
            pltpu.VMEM((paths, hidden), BF16),
            pltpu.VMEM((CHIPS, 2 * depth, hidden), F32),
            pltpu.VMEM((CHIPS, depth, hidden), BF16),
            pltpu.VMEM((CHIPS, depth, hidden), BF16),
            pltpu.VMEM((CHIPS, depth, hidden), BF16),
            pltpu.VMEM((2, CHIPS, depth, hidden), BF16),
            pltpu.VMEM((8, paths), F32),
            pltpu.VMEM((dates, 8, paths), F32),
            pltpu.VMEM((paths, 8), F32),
            pltpu.VMEM((24, hidden), F32),
            pltpu.VMEM((24, hidden), F32),
            pltpu.VMEM((CHIPS, 24, hidden // 2), F32),
            pltpu.VMEM((24, hidden), F32),
            dma((dates,)),
            dma((dates,)),
            dma((3, 2 * CHIPS, part_count)),
            dma((2 * CHIPS, part_count)),
            dma((CHIPS,)),
            dma((CHIPS,)),
            dma((CHIPS, part_count)),
            dma((2, CHIPS, part_count)),
            dma,
            dma,
            dma((CHIPS - 1,)),
            dma((CHIPS,)),
            dma,
            dma,
        ],
        compiler_params=pltpu.CompilerParams(collective_id=0, has_side_effects=True),
        cost_estimate=pl.CostEstimate(
            flops=6 * paths * hidden * hidden, bytes_accessed=4 * hidden * hidden, transcendentals=0
        ),
    )(level_range, factors, payoff, terminal, decisions, w_first, vectors, shard)


def update_kernel(
    mid_ref,
    small_ref,
    w_in_ref,
    w_mid_ref,
    vec_ref,
    mom_in_ref,
    mom_mid_ref,
    mom_vec_ref,
    value_ref,
    new_w_in_ref,
    new_w_mid_ref,
    new_vec_ref,
    new_mom_in_ref,
    new_mom_mid_ref,
    new_mom_vec_ref,
    new_in_copy_ref,
    new_mid_copy_ref,
    *,
    paths_total,
):
    value_ref[0] = jnp.sum(small_ref[19:20, :]) / paths_total

    def update(grad, master, momentum, new_master, new_momentum, at):
        moved = MOMENTUM * momentum[0, at, :] + grad
        new_momentum[0, at, :] = moved
        stepped = master[0, at, :] - STEP_SIZE * moved
        new_master[0, at, :] = stepped
        return stepped

    factors = w_in_ref.shape[1]
    everything = pl.ds(0, factors)
    stepped = update(
        small_ref[0:factors, :], w_in_ref, mom_in_ref, new_w_in_ref, new_mom_in_ref, everything
    )
    new_in_copy_ref[0] = stepped.astype(BF16)
    for row in range(vec_ref.shape[0]):
        at_row = small_ref[factors + row : factors + row + 1, :]
        moved = MOMENTUM * mom_vec_ref[row] + at_row
        new_mom_vec_ref[row] = moved
        new_vec_ref[row] = vec_ref[row] - STEP_SIZE * moved
    rows = 16

    def body(i, carry):
        at = pl.ds(pl.multiple_of(i * rows, rows), rows)
        stepped = update(
            mid_ref[at, :], w_mid_ref, mom_mid_ref, new_w_mid_ref, new_mom_mid_ref, at
        )
        new_mid_copy_ref[0, at, :] = stepped.astype(BF16)
        return carry

    lax.fori_loop(0, mid_ref.shape[0] // rows, body, 0)


def shards(
    factors,
    payoff,
    terminal,
    decisions,
    level_range,
    w_in_master,
    w_mid_master,
    vec_master,
    w_in_copy,
    w_mid_copy,
    mom_in,
    mom_mid,
    mom_vec,
):
    paths_total = payoff.shape[1] * lax.axis_size("path")
    vectors = jnp.swapaxes(vec_master, 0, 1)
    mom_rows = jnp.swapaxes(mom_vec, 0, 1)
    mid_grad, small = run_step(
        level_range.T, factors, payoff, terminal, decisions, w_in_copy, vectors, w_mid_copy
    )
    like = jax.ShapeDtypeStruct
    vmem = pl.BlockSpec(memory_space=pltpu.VMEM)
    outs = pl.pallas_call(
        functools.partial(update_kernel, paths_total=paths_total),
        out_shape=(
            like((1,), F32),
            like(w_in_master.shape, F32),
            like(w_mid_master.shape, F32),
            like(vectors.shape, F32),
            like(w_in_master.shape, F32),
            like(w_mid_master.shape, F32),
            like(vectors.shape, F32),
            like(w_in_master.shape, BF16),
            like(w_mid_master.shape, BF16),
        ),
        in_specs=[vmem] * 8,
        out_specs=(pl.BlockSpec(memory_space=pltpu.SMEM),) + (vmem,) * 8,
    )(mid_grad, small, w_in_master, w_mid_master, vectors, mom_in, mom_mid, mom_rows)
    return tuple(jnp.swapaxes(out, 0, 1) if at in (3, 6) else out for at, out in enumerate(outs))


def solution(mesh):
    in_specs = (
        P(None, "path"),
        P(None, "path"),
        P("vol", "path"),
        P(None, "vol", "path"),
        P(),
        P("vol", None, None),
        P("vol", "path", None),
        P("vol", None, None),
        P("vol", None, None),
        P("vol", "path", None),
        P("vol", None, None),
        P("vol", "path", None),
        P("vol", None, None),
    )
    out_specs = (
        P("vol"),
        P("vol", None, None),
        P("vol", "path", None),
        P("vol", None, None),
        P("vol", None, None),
        P("vol", "path", None),
        P("vol", None, None),
        P("vol", None, None),
        P("vol", "path", None),
    )
    return jax.shard_map(shards, mesh=mesh, in_specs=in_specs, out_specs=out_specs, check_vma=False)
```

```python
import functools

import jax
import jax.numpy as jnp
from jax import lax
from jax.experimental import pallas as pl
from jax.experimental.pallas import tpu as pltpu
from jax.sharding import PartitionSpec as P

MOMENTUM = 0.9
STEP_SIZE = 0.01
CHIPS = 4
HALVES = 2
F32 = jnp.float32
BF16 = jnp.bfloat16
ORDER = ((3, 2, 1, 0), (3, 0, 2, 1), (0, 3, 1, 2), (0, 1, 2, 3))


def sigmoid(u):
    return 0.5 * jnp.tanh(0.5 * u) + 0.5


def step_kernel(
    range_ref,
    fac_ref,
    payoff_ref,
    terminal_ref,
    decisions_ref,
    win_ref,
    vec_ref,
    shard_ref,
    mid_ref,
    small_ref,
    wfull,
    h1,
    h1t,
    slope,
    pre2,
    d2,
    grads,
    to_pair,
    from_pair,
    to_line,
    from_line,
    level_out,
    level_in,
    gain_col,
    small,
    small_pair,
    small_chip,
    small_sum,
    level_send,
    level_recv,
    ag_send,
    ag_recv,
    pair_send,
    pair_recv,
    line_send,
    line_recv,
    small_send,
    small_recv,
    chip_send,
    chip_recv,
    sum_send,
    sum_recv,
):
    level = lax.axis_index("vol")
    levels = lax.axis_size("vol")
    dates = payoff_ref.shape[0]
    me = lax.axis_index("path")
    c = me // 2
    k = me % 2
    other = me + 1 - 2 * k
    hidden = h1.shape[1]
    paths = h1.shape[0]
    depth = shard_ref.shape[1]
    part = depth // HALVES
    half_columns = hidden // 2

    def remote(src, dst, send, recv, to):
        return pltpu.make_async_remote_copy(
            src_ref=src,
            dst_ref=dst,
            send_sem=send,
            recv_sem=recv,
            device_id={"path": to},
            device_id_type=pl.DeviceIdType.MESH,
        )

    barrier = pltpu.get_barrier_semaphore()

    def greet_level(to):
        pl.semaphore_signal(
            barrier, inc=1, device_id={"vol": to}, device_id_type=pl.DeviceIdType.MESH
        )

    def each_level(above, below):
        for back in range(1, dates + 1):
            pl.when(level + back < levels)(functools.partial(above, back))
            pl.when(level >= back)(functools.partial(below, back))

    each_level(lambda back: greet_level(level + back), lambda back: greet_level(level - back))
    pl.semaphore_signal(barrier, inc=1, device_id={"path": other}, device_id_type=pl.DeviceIdType.MESH)
    for far in range(1, CHIPS):
        pl.semaphore_signal(
            barrier,
            inc=1,
            device_id={"path": ((c + far) % CHIPS) * 2 + k},
            device_id_type=pl.DeviceIdType.MESH,
        )

    level_out[0:1, :] = terminal_ref[...]
    for date in range(1, dates):
        level_out[date : date + 1, :] = decisions_ref[date - 1].astype(F32)

    def level_copy(back):
        return pltpu.make_async_remote_copy(
            src_ref=level_out,
            dst_ref=level_in.at[back - 1],
            send_sem=level_send.at[back - 1],
            recv_sem=level_recv.at[back - 1],
            device_id={"vol": level + back},
            device_id_type=pl.DeviceIdType.MESH,
        )

    rows_first = 128

    def first_layer(m, carry):
        at = pl.ds(pl.multiple_of(m * rows_first, rows_first), rows_first)
        pre = (
            lax.dot_general(
                fac_ref[:, at], win_ref[0], (((0,), (0,)), ((), ())), preferred_element_type=F32
            )
            + vec_ref[0]
        )
        s = sigmoid(pre)
        act = pre * s
        slope[at, :] = s * (1.0 + pre * (1.0 - s))
        h1[at, :] = act.astype(BF16)
        h1t[:, at] = jnp.transpose(act).astype(BF16)
        return carry

    tiles_first = paths // rows_first
    tiles_ahead = tiles_first // 2
    lax.fori_loop(0, tiles_ahead, first_layer, 0)
    peers = CHIPS
    for back in range(1, dates + 1):
        peers = peers + jnp.where(level + back < levels, 1, 0) + jnp.where(level >= back, 1, 0)
    pl.semaphore_wait(barrier, peers)

    def rows_of(slot, h):
        return pl.ds(pl.multiple_of(slot * depth + h * part, part), part)

    LEFT, RIGHT, PAIR = 0, 1, 2

    def gather_copy(source, slot, h, way, to):
        return remote(
            source, wfull.at[rows_of(slot, h), :], ag_send.at[way, slot, h], ag_recv.at[slot, h], to
        )

    def shard_part(h):
        return shard_ref.at[0, pl.ds(h * part, part), :]

    for h in range(HALVES):

        @pl.when(c > 0)
        def _():
            gather_copy(shard_part(h), me, h, LEFT, me - 2).start()

        @pl.when(c < CHIPS - 1)
        def _():
            gather_copy(shard_part(h), me, h, RIGHT, me + 2).start()

    for h in range(HALVES):
        gather_copy(shard_part(h), me, h, PAIR, other).start()
    wfull[pl.ds(pl.multiple_of(me * depth, depth), depth), :] = shard_ref[0]

    def no_level(back):
        level_in[back - 1] = jnp.zeros(level_in.shape[1:], F32)

    for back in range(1, dates + 1):
        pl.when(level + back < levels)(level_copy(back).start)
        pl.when(level < back)(functools.partial(no_level, back))
    lax.fori_loop(tiles_ahead, tiles_first, first_layer, 0)

    def landed(slot, h):
        at = wfull.at[rows_of(slot, h), :]
        gather_copy(at, slot, h, PAIR, other).wait_recv()

    def forward(slot, h, way, to):
        gather_copy(wfull.at[rows_of(slot, h), :], slot, h, way, to).start()

    def relay(far):
        for h in range(HALVES):

            @pl.when(c >= far)
            def _():
                slot = me - 2 * far
                landed(slot, h)

                @pl.when(c < CHIPS - 1)
                def _():
                    forward(slot, h, RIGHT, me + 2)

                forward(slot, h, PAIR, other)

            @pl.when(c + far < CHIPS)
            def _():
                slot = me + 2 * far
                landed(slot, h)

                @pl.when(c > 0)
                def _():
                    forward(slot, h, LEFT, me - 2)

                forward(slot, h, PAIR, other)

    tile = 256

    def middle(chip, first):
        columns = pl.ds(pl.multiple_of(chip * 2 * depth, 2 * depth), 2 * depth)

        def body(m, carry):
            at = pl.ds(pl.multiple_of(m * tile, tile), tile)
            product = jnp.dot(h1[at, columns], wfull[columns, :], preferred_element_type=F32)
            if first:
                pre2[at, :] = product + vec_ref[1]
            else:
                pre2[at, :] += product
            return carry

        lax.fori_loop(0, paths // tile, body, 0)

    def absorb(far):
        @pl.when(c >= far)
        def _():
            for h in range(HALVES):
                landed(other - 2 * far, h)
            middle(c - far, False)

        @pl.when(c + far < CHIPS)
        def _():
            for h in range(HALVES):
                landed(other + 2 * far, h)
            middle(c + far, False)

    relay(1)
    for h in range(HALVES):
        landed(other, h)
    middle(c, True)
    absorb(1)
    relay(2)

    for back in range(1, dates + 1):
        pl.when(level >= back)(level_copy(back).wait_recv)

    def of_level(back, row):
        if back == 0:
            return level_out[row : row + 1, :]
        return level_in[back - 1, row : row + 1, :]

    carry = [of_level(back, 0) for back in range(dates + 1)]
    for date in range(dates - 1, 0, -1):
        lower_end, upper_end = range_ref[0, date], range_ref[1, date]
        after = []
        for back in range(len(carry) - 1):
            here = level - back
            inside = jnp.logical_and(here >= lower_end, here <= upper_end)
            free = jnp.where(inside, of_level(back, date), 0.0)
            taken = jnp.where(here > upper_end, 1.0, free)
            paid = payoff_ref[date : date + 1, :] + carry[back + 1]
            after.append(taken * paid + (1.0 - taken) * carry[back])
        carry = after
    gain_row = payoff_ref[0:1, :] + carry[1] - carry[0]
    active = jnp.logical_and(level >= range_ref[0, 0], level <= range_ref[1, 0])
    rest_row = jnp.where(level > range_ref[1, 0], gain_row, 0.0) + carry[0]
    gain_active = jnp.where(active, gain_row, 0.0)
    gain_col[...] = jnp.transpose(jnp.broadcast_to(gain_active, (8, paths)))
    small[19:20, :] = rest_row
    absorb(2)
    relay(3)
    absorb(3)

    rows_second = 128

    def second_layer(m, carry):
        bias_two, head, value = carry
        at = pl.ds(pl.multiple_of(m * rows_second, rows_second), rows_second)
        pre = pre2[at, :]
        s = sigmoid(pre)
        act = (pre * s).astype(BF16).astype(F32)
        weights = vec_ref[2]
        chance = sigmoid(jnp.sum(act * weights, axis=1, keepdims=True))
        gain = gain_col[at, 0:1]
        d_logit = -gain * chance * (1.0 - chance)
        d_pre = d_logit * weights * (s * (1.0 + pre * (1.0 - s)))
        d2[at, :] = d_pre.astype(BF16)
        bias_two = bias_two + jnp.sum(d_pre, axis=0, keepdims=True)
        head = head + jnp.sum(d_logit * act, axis=0, keepdims=True)
        value = value + jnp.sum(chance * gain, axis=0, keepdims=True)
        return bias_two, head, value

    zero_row = jnp.zeros((1, hidden), F32)
    bias_two, head, value = lax.fori_loop(
        0, paths // rows_second, second_layer, (zero_row, zero_row, jnp.zeros((1, 1), F32))
    )
    small[17:18, :] = bias_two
    small[18:19, :] = head
    lane = lax.broadcasted_iota(jnp.int32, (1, hidden), 1)
    small[19:20, :] += jnp.where(lane == 0, value, 0.0)
    small[20:24, :] = jnp.zeros((4, hidden), F32)

    def order(step):
        packed = sum(ORDER[chip][step] * 4**chip for chip in range(CHIPS))
        return lax.rem(lax.shift_right_logical(jnp.int32(packed), 2 * c), jnp.int32(4))

    def pair_copy(e):
        return remote(to_pair.at[e], from_pair.at[e], pair_send.at[e], pair_recv.at[e], other)

    def product(step):
        e = order(step)
        rows = pl.ds(pl.multiple_of(e * 2 * depth, 2 * depth), 2 * depth)

        def body(n, carry):
            at = pl.ds(pl.multiple_of(n * tile, tile), tile)
            grads[e, :, at] = jnp.dot(h1t[rows, :], d2[:, at], preferred_element_type=F32)
            return carry

        lax.fori_loop(0, hidden // tile, body, 0)
        theirs = pl.ds(pl.multiple_of((1 - k) * depth, depth), depth)
        to_pair[e] = grads[e, theirs, :].astype(BF16)
        pair_copy(e).start()

    def line_copy(way, e, h, to):
        at = pl.ds(h * part, part)
        return remote(
            to_line.at[e, at, :],
            from_line.at[way, e, at, :],
            line_send.at[e, h],
            line_recv.at[way, e, h],
            to,
        )

    def own_part(e, h):
        mine = pl.ds(pl.multiple_of(k * depth + h * part, part), part)
        return grads[e, mine, :] + from_pair[e, pl.ds(h * part, part), :].astype(F32)

    def along_line(step, halves=range(HALVES)):
        e = order(step)
        if 0 in halves:
            pair_copy(e).wait_recv()
        for h in halves:
            at = pl.ds(h * part, part)

            @pl.when(e > c)
            def _():
                @pl.when(c == 0)
                def _():
                    to_line[e, at, :] = own_part(e, h).astype(BF16)

                @pl.when(c > 0)
                def _():
                    line_copy(0, e, h, other).wait_recv()
                    total = own_part(e, h) + from_line[0, e, at, :].astype(F32)
                    to_line[e, at, :] = total.astype(BF16)

                line_copy(0, e, h, me + 2).start()

            @pl.when(e < c)
            def _():
                @pl.when(c == CHIPS - 1)
                def _():
                    to_line[e, at, :] = own_part(e, h).astype(BF16)

                @pl.when(c < CHIPS - 1)
                def _():
                    line_copy(1, e, h, other).wait_recv()
                    total = own_part(e, h) + from_line[1, e, at, :].astype(F32)
                    to_line[e, at, :] = total.astype(BF16)

                line_copy(1, e, h, me - 2).start()

    at_end = c * (CHIPS - 1 - c) == 0
    product(0)
    product(1)
    pl.when(at_end)(lambda: along_line(0))
    product(2)
    pl.when(at_end)(lambda: along_line(1))
    product(3)
    pl.when(at_end)(lambda: along_line(2))

    def back(m, carry):
        bias_one, first = carry
        at = pl.ds(pl.multiple_of(m * tile, tile), tile)
        d_pre = (
            lax.dot_general(
                d2[at, :], wfull[...], (((1,), (1,)), ((), ())), preferred_element_type=F32
            )
            * slope[at, :]
        )
        bias_one = bias_one + jnp.sum(d_pre, axis=0, keepdims=True)
        first = first + jnp.dot(fac_ref[:, at], d_pre.astype(BF16), preferred_element_type=F32)
        return bias_one, first

    def on_the_way(step, h):
        pl.when(jnp.logical_not(at_end))(lambda: along_line(step, (h,)))

    sums = (zero_row, jnp.zeros((fac_ref.shape[0], hidden), F32))
    sums = lax.fori_loop(0, paths // tile // 2, back, sums)
    on_the_way(0, 0)
    bias_one, first = lax.fori_loop(paths // tile // 2, paths // tile, back, sums)
    small[0:16, :] = first
    small[16:17, :] = bias_one

    my_columns = pl.ds(pl.multiple_of(k * half_columns, half_columns), half_columns)
    their_columns = pl.ds(pl.multiple_of((1 - k) * half_columns, half_columns), half_columns)
    pair_sum = remote(small, small_pair, small_send, small_recv, other)
    pair_sum.start()
    on_the_way(0, 1)
    pair_sum.wait_recv()
    small_chip[c] = small[:, my_columns] + small_pair[:, my_columns]

    def chip_copy(far):
        to = ((c + far) % CHIPS) * 2 + k
        return remote(
            small_chip.at[c], small_chip.at[c], chip_send.at[far - 1], chip_recv.at[c], to
        )

    def chip_landed(far):
        chip = (c + far) % CHIPS
        slot = small_chip.at[chip]
        remote(slot, slot, chip_send.at[far - 1], chip_recv.at[chip], other).wait_recv()

    for far in range(1, CHIPS):
        chip_copy(far).start()
    for h in range(HALVES):
        for step in (1, 2):
            on_the_way(step, h)
    for far in range(1, CHIPS):
        chip_landed(far)
    small_sum[:, my_columns] = small_chip[0] + small_chip[1] + small_chip[2] + small_chip[3]
    mine = small_sum.at[:, my_columns]
    theirs = small_sum.at[:, their_columns]
    share = remote(mine, mine, sum_send, sum_recv, other)
    share.start()

    pair_copy(c).wait_recv()
    for h in range(HALVES):
        mid_ref[pl.ds(h * part, part), :] = own_part(c, h)

    def arrived(way):
        for h in range(HALVES):
            at = pl.ds(h * part, part)
            line_copy(way, c, h, other).wait_recv()
            mid_ref[at, :] += from_line[way, c, at, :].astype(F32)

    pl.when(c > 0)(lambda: arrived(0))
    pl.when(c < CHIPS - 1)(lambda: arrived(1))
    remote(theirs, theirs, sum_send, sum_recv, other).wait_recv()
    small_ref[...] = small_sum[...]

    for back in range(1, dates + 1):
        pl.when(level + back < levels)(level_copy(back).wait_send)
    for h in range(HALVES):
        gather_copy(shard_part(h), me, h, PAIR, other).wait_send()

        @pl.when(c > 0)
        def _():
            gather_copy(shard_part(h), me, h, LEFT, me - 2).wait_send()

        @pl.when(c < CHIPS - 1)
        def _():
            gather_copy(shard_part(h), me, h, RIGHT, me + 2).wait_send()

        for far in range(1, CHIPS):

            @pl.when(c >= far)
            def _():
                slot = me - 2 * far
                source = wfull.at[rows_of(slot, h), :]
                gather_copy(source, slot, h, PAIR, other).wait_send()

                @pl.when(c < CHIPS - 1)
                def _():
                    gather_copy(source, slot, h, RIGHT, me + 2).wait_send()

            @pl.when(c + far < CHIPS)
            def _():
                slot = me + 2 * far
                source = wfull.at[rows_of(slot, h), :]
                gather_copy(source, slot, h, PAIR, other).wait_send()

                @pl.when(c > 0)
                def _():
                    gather_copy(source, slot, h, LEFT, me - 2).wait_send()

    for e in range(CHIPS):
        pair_copy(e).wait_send()
    for step in range(CHIPS - 1):
        for h in range(HALVES):
            line_copy(0, order(step), h, other).wait_send()
    pair_sum.wait_send()
    for far in range(1, CHIPS):
        chip_copy(far).wait_send()
    share.wait_send()


def run_step(level_range, factors, payoff, terminal, decisions, w_first, vectors, shard):
    paths = factors.shape[1]
    dates = payoff.shape[0]
    _, depth, hidden = shard.shape
    part_count = HALVES
    dma = pltpu.SemaphoreType.DMA
    vmem = pl.BlockSpec(memory_space=pltpu.VMEM)
    return pl.pallas_call(
        step_kernel,
        out_shape=(
            jax.ShapeDtypeStruct((depth, hidden), F32),
            jax.ShapeDtypeStruct((24, hidden), F32),
        ),
        in_specs=[pl.BlockSpec(memory_space=pltpu.SMEM)] + [vmem] * 7,
        out_specs=(vmem, vmem),
        scratch_shapes=[
            pltpu.VMEM((hidden, hidden), BF16),
            pltpu.VMEM((paths, hidden), BF16),
            pltpu.VMEM((hidden, paths), BF16),
            pltpu.VMEM((paths, hidden), F32),
            pltpu.VMEM((paths, hidden), F32),
            pltpu.VMEM((paths, hidden), BF16),
            pltpu.VMEM((CHIPS, 2 * depth, hidden), F32),
            pltpu.VMEM((CHIPS, depth, hidden), BF16),
            pltpu.VMEM((CHIPS, depth, hidden), BF16),
            pltpu.VMEM((CHIPS, depth, hidden), BF16),
            pltpu.VMEM((2, CHIPS, depth, hidden), BF16),
            pltpu.VMEM((8, paths), F32),
            pltpu.VMEM((dates, 8, paths), F32),
            pltpu.VMEM((paths, 8), F32),
            pltpu.VMEM((24, hidden), F32),
            pltpu.VMEM((24, hidden), F32),
            pltpu.VMEM((CHIPS, 24, hidden // 2), F32),
            pltpu.VMEM((24, hidden), F32),
            dma((dates,)),
            dma((dates,)),
            dma((3, 2 * CHIPS, part_count)),
            dma((2 * CHIPS, part_count)),
            dma((CHIPS,)),
            dma((CHIPS,)),
            dma((CHIPS, part_count)),
            dma((2, CHIPS, part_count)),
            dma,
            dma,
            dma((CHIPS - 1,)),
            dma((CHIPS,)),
            dma,
            dma,
        ],
        compiler_params=pltpu.CompilerParams(collective_id=0, has_side_effects=True),
        cost_estimate=pl.CostEstimate(
            flops=6 * paths * hidden * hidden, bytes_accessed=4 * hidden * hidden, transcendentals=0
        ),
    )(level_range, factors, payoff, terminal, decisions, w_first, vectors, shard)


def update_kernel(
    mid_ref,
    small_ref,
    w_in_ref,
    w_mid_ref,
    vec_ref,
    mom_in_ref,
    mom_mid_ref,
    mom_vec_ref,
    value_ref,
    new_w_in_ref,
    new_w_mid_ref,
    new_vec_ref,
    new_mom_in_ref,
    new_mom_mid_ref,
    new_mom_vec_ref,
    new_in_copy_ref,
    new_mid_copy_ref,
    *,
    paths_total,
):
    value_ref[0] = jnp.sum(small_ref[19:20, :]) / paths_total

    def update(grad, master, momentum, new_master, new_momentum, at):
        moved = MOMENTUM * momentum[0, at, :] + grad
        new_momentum[0, at, :] = moved
        stepped = master[0, at, :] - STEP_SIZE * moved
        new_master[0, at, :] = stepped
        return stepped

    factors = w_in_ref.shape[1]
    everything = pl.ds(0, factors)
    stepped = update(
        small_ref[0:factors, :], w_in_ref, mom_in_ref, new_w_in_ref, new_mom_in_ref, everything
    )
    new_in_copy_ref[0] = stepped.astype(BF16)
    for row in range(vec_ref.shape[0]):
        at_row = small_ref[factors + row : factors + row + 1, :]
        moved = MOMENTUM * mom_vec_ref[row] + at_row
        new_mom_vec_ref[row] = moved
        new_vec_ref[row] = vec_ref[row] - STEP_SIZE * moved
    rows = 16

    def body(i, carry):
        at = pl.ds(pl.multiple_of(i * rows, rows), rows)
        stepped = update(
            mid_ref[at, :], w_mid_ref, mom_mid_ref, new_w_mid_ref, new_mom_mid_ref, at
        )
        new_mid_copy_ref[0, at, :] = stepped.astype(BF16)
        return carry

    lax.fori_loop(0, mid_ref.shape[0] // rows, body, 0)


def shards(
    factors,
    payoff,
    terminal,
    decisions,
    level_range,
    w_in_master,
    w_mid_master,
    vec_master,
    w_in_copy,
    w_mid_copy,
    mom_in,
    mom_mid,
    mom_vec,
):
    paths_total = payoff.shape[1] * lax.axis_size("path")
    vectors = jnp.swapaxes(vec_master, 0, 1)
    mom_rows = jnp.swapaxes(mom_vec, 0, 1)
    mid_grad, small = run_step(
        level_range.T, factors, payoff, terminal, decisions, w_in_copy, vectors, w_mid_copy
    )
    like = jax.ShapeDtypeStruct
    vmem = pl.BlockSpec(memory_space=pltpu.VMEM)
    outs = pl.pallas_call(
        functools.partial(update_kernel, paths_total=paths_total),
        out_shape=(
            like((1,), F32),
            like(w_in_master.shape, F32),
            like(w_mid_master.shape, F32),
            like(vectors.shape, F32),
            like(w_in_master.shape, F32),
            like(w_mid_master.shape, F32),
            like(vectors.shape, F32),
            like(w_in_master.shape, BF16),
            like(w_mid_master.shape, BF16),
        ),
        in_specs=[vmem] * 8,
        out_specs=(pl.BlockSpec(memory_space=pltpu.SMEM),) + (vmem,) * 8,
    )(mid_grad, small, w_in_master, w_mid_master, vectors, mom_in, mom_mid, mom_rows)
    return tuple(jnp.swapaxes(out, 0, 1) if at in (3, 6) else out for at, out in enumerate(outs))


def solution(mesh):
    in_specs = (
        P(None, "path"),
        P(None, "path"),
        P("vol", "path"),
        P(None, "vol", "path"),
        P(),
        P("vol", None, None),
        P("vol", "path", None),
        P("vol", None, None),
        P("vol", None, None),
        P("vol", "path", None),
        P("vol", None, None),
        P("vol", "path", None),
        P("vol", None, None),
    )
    out_specs = (
        P("vol"),
        P("vol", None, None),
        P("vol", "path", None),
        P("vol", None, None),
        P("vol", None, None),
        P("vol", "path", None),
        P("vol", None, None),
        P("vol", None, None),
        P("vol", "path", None),
    )
    return jax.shard_map(shards, mesh=mesh, in_specs=in_specs, out_specs=out_specs, check_vma=False)
```

```python
import functools

import jax
import jax.numpy as jnp
from jax import lax
from jax.experimental import pallas as pl
from jax.experimental.pallas import tpu as pltpu
from jax.sharding import PartitionSpec as P

MOMENTUM = 0.9
STEP_SIZE = 0.01
CHIPS = 4
HALVES = 2
F32 = jnp.float32
BF16 = jnp.bfloat16
ORDER = ((3, 2, 1, 0), (3, 0, 2, 1), (0, 3, 1, 2), (0, 1, 2, 3))


def sigmoid(u):
    return 0.5 * jnp.tanh(0.5 * u) + 0.5


def step_kernel(
    range_ref,
    fac_far,
    payoff_far,
    terminal_far,
    decisions_far,
    win_far,
    vec_far,
    shard_far,
    mid_ref,
    small_ref,
    fac_ref,
    payoff_ref,
    terminal_ref,
    decisions_ref,
    win_ref,
    vec_ref,
    shard_ref,
    fetched,
    wfull,
    h1,
    h1t,
    slope,
    pre2,
    d2,
    grads,
    to_pair,
    from_pair,
    to_line,
    from_line,
    level_out,
    level_in,
    gain_col,
    small,
    small_pair,
    small_chip,
    small_sum,
    level_send,
    level_recv,
    ag_send,
    ag_recv,
    pair_send,
    pair_recv,
    line_send,
    line_recv,
    small_send,
    small_recv,
    chip_send,
    chip_recv,
    sum_send,
    sum_recv,
):
    level = lax.axis_index("vol")
    levels = lax.axis_size("vol")
    dates = payoff_ref.shape[0]
    me = lax.axis_index("path")
    c = me // 2
    k = me % 2
    other = me + 1 - 2 * k
    hidden = h1.shape[1]
    paths = h1.shape[0]
    depth = shard_ref.shape[1]
    part = depth // HALVES
    half_columns = hidden // 2

    def remote(src, dst, send, recv, to):
        return pltpu.make_async_remote_copy(
            src_ref=src,
            dst_ref=dst,
            send_sem=send,
            recv_sem=recv,
            device_id={"path": to},
            device_id_type=pl.DeviceIdType.MESH,
        )

    fetches = [
        pltpu.make_async_copy(far, near, fetched.at[at])
        for at, (far, near) in enumerate(
            (
                (terminal_far, terminal_ref),
                (decisions_far, decisions_ref),
                (fac_far, fac_ref),
                (win_far, win_ref),
                (vec_far, vec_ref),
                (payoff_far, payoff_ref),
                (shard_far, shard_ref),
            )
        )
    ]
    for fetch in fetches:
        fetch.start()
    barrier = pltpu.get_barrier_semaphore()

    def greet_level(to):
        pl.semaphore_signal(
            barrier, inc=1, device_id={"vol": to}, device_id_type=pl.DeviceIdType.MESH
        )

    def each_level(above, below):
        for back in range(1, dates + 1):
            pl.when(level + back < levels)(functools.partial(above, back))
            pl.when(level >= back)(functools.partial(below, back))

    each_level(lambda back: greet_level(level + back), lambda back: greet_level(level - back))
    pl.semaphore_signal(barrier, inc=1, device_id={"path": other}, device_id_type=pl.DeviceIdType.MESH)
    for far in range(1, CHIPS):
        pl.semaphore_signal(
            barrier,
            inc=1,
            device_id={"path": ((c + far) % CHIPS) * 2 + k},
            device_id_type=pl.DeviceIdType.MESH,
        )

    for fetch in fetches:
        fetch.wait()
    level_out[0:1, :] = terminal_ref[...]
    for date in range(1, dates):
        level_out[date : date + 1, :] = decisions_ref[date - 1].astype(F32)

    def level_copy(back):
        return pltpu.make_async_remote_copy(
            src_ref=level_out,
            dst_ref=level_in.at[back - 1],
            send_sem=level_send.at[back - 1],
            recv_sem=level_recv.at[back - 1],
            device_id={"vol": level + back},
            device_id_type=pl.DeviceIdType.MESH,
        )

    rows_first = 128

    def first_layer(m, carry):
        at = pl.ds(pl.multiple_of(m * rows_first, rows_first), rows_first)
        pre = (
            lax.dot_general(
                fac_ref[:, at], win_ref[0], (((0,), (0,)), ((), ())), preferred_element_type=F32
            )
            + vec_ref[0]
        )
        s = sigmoid(pre)
        act = pre * s
        slope[at, :] = s + act * (1.0 - s)
        h1[at, :] = act.astype(BF16)
        h1t[:, at] = jnp.transpose(act).astype(BF16)
        return carry

    tiles_first = paths // rows_first
    tiles_ahead = tiles_first // 2
    lax.fori_loop(0, tiles_ahead, first_layer, 0)
    peers = CHIPS
    for back in range(1, dates + 1):
        peers = peers + jnp.where(level + back < levels, 1, 0) + jnp.where(level >= back, 1, 0)
    pl.semaphore_wait(barrier, peers)

    def rows_of(slot, h):
        return pl.ds(pl.multiple_of(slot * depth + h * part, part), part)

    LEFT, RIGHT, PAIR = 0, 1, 2

    def gather_copy(source, slot, h, way, to):
        return remote(
            source, wfull.at[rows_of(slot, h), :], ag_send.at[way, slot, h], ag_recv.at[slot, h], to
        )

    def shard_part(h):
        return shard_ref.at[0, pl.ds(h * part, part), :]

    for h in range(HALVES):

        @pl.when(c > 0)
        def _():
            gather_copy(shard_part(h), me, h, LEFT, me - 2).start()

        @pl.when(c < CHIPS - 1)
        def _():
            gather_copy(shard_part(h), me, h, RIGHT, me + 2).start()

    for h in range(HALVES):
        gather_copy(shard_part(h), me, h, PAIR, other).start()
    wfull[pl.ds(pl.multiple_of(me * depth, depth), depth), :] = shard_ref[0]

    def no_level(back):
        level_in[back - 1] = jnp.zeros(level_in.shape[1:], F32)

    for back in range(1, dates + 1):
        pl.when(level + back < levels)(level_copy(back).start)
        pl.when(level < back)(functools.partial(no_level, back))
    lax.fori_loop(tiles_ahead, tiles_first, first_layer, 0)

    def landed(slot, h):
        at = wfull.at[rows_of(slot, h), :]
        gather_copy(at, slot, h, PAIR, other).wait_recv()

    def forward(slot, h, way, to):
        gather_copy(wfull.at[rows_of(slot, h), :], slot, h, way, to).start()

    def relay(far):
        for h in range(HALVES):

            @pl.when(c >= far)
            def _():
                slot = me - 2 * far
                landed(slot, h)

                @pl.when(c < CHIPS - 1)
                def _():
                    forward(slot, h, RIGHT, me + 2)

                forward(slot, h, PAIR, other)

            @pl.when(c + far < CHIPS)
            def _():
                slot = me + 2 * far
                landed(slot, h)

                @pl.when(c > 0)
                def _():
                    forward(slot, h, LEFT, me - 2)

                forward(slot, h, PAIR, other)

    tile = 256

    def middle(chip, first):
        columns = pl.ds(pl.multiple_of(chip * 2 * depth, 2 * depth), 2 * depth)

        def body(m, carry):
            at = pl.ds(pl.multiple_of(m * tile, tile), tile)
            product = jnp.dot(h1[at, columns], wfull[columns, :], preferred_element_type=F32)
            if first:
                pre2[at, :] = product + vec_ref[1]
            else:
                pre2[at, :] += product
            return carry

        lax.fori_loop(0, paths // tile, body, 0)

    def absorb(far):
        @pl.when(c >= far)
        def _():
            for h in range(HALVES):
                landed(other - 2 * far, h)
            middle(c - far, False)

        @pl.when(c + far < CHIPS)
        def _():
            for h in range(HALVES):
                landed(other + 2 * far, h)
            middle(c + far, False)

    at_end = c * (CHIPS - 1 - c) == 0
    relay(1)
    for h in range(HALVES):
        landed(other, h)
    middle(c, True)
    absorb(1)
    relay(2)

    for back in range(1, dates + 1):
        pl.when(level >= back)(level_copy(back).wait_recv)

    def of_level(back, row):
        if back == 0:
            return level_out[row : row + 1, :]
        return level_in[back - 1, row : row + 1, :]

    carry = [of_level(back, 0) for back in range(dates + 1)]
    for date in range(dates - 1, 0, -1):
        lower_end, upper_end = range_ref[0, date], range_ref[1, date]
        after = []
        for back in range(len(carry) - 1):
            here = level - back
            inside = jnp.logical_and(here >= lower_end, here <= upper_end)
            free = jnp.where(inside, of_level(back, date), 0.0)
            taken = jnp.where(here > upper_end, 1.0, free)
            paid = payoff_ref[date : date + 1, :] + carry[back + 1]
            after.append(taken * paid + (1.0 - taken) * carry[back])
        carry = after
    gain_row = payoff_ref[0:1, :] + carry[1] - carry[0]
    active = jnp.logical_and(level >= range_ref[0, 0], level <= range_ref[1, 0])
    rest_row = jnp.where(level > range_ref[1, 0], gain_row, 0.0) + carry[0]
    gain_active = jnp.where(active, gain_row, 0.0)
    gain_col[...] = jnp.transpose(jnp.broadcast_to(gain_active, (8, paths)))
    small[19:20, :] = rest_row
    pl.when(at_end)(lambda: absorb(2))
    relay(3)
    last = (CHIPS - 1) * (1 - c // 2)
    for h in range(HALVES):
        landed(other + 2 * (last - c), h)
    last_columns = pl.ds(pl.multiple_of(last * 2 * depth, 2 * depth), 2 * depth)

    rows_second = 128

    def second_layer(m, carry):
        bias_two, head, value = carry
        at = pl.ds(pl.multiple_of(m * rows_second, rows_second), rows_second)
        pre = pre2[at, :] + jnp.dot(
            h1[at, last_columns], wfull[last_columns, :], preferred_element_type=F32
        )
        s = sigmoid(pre)
        silu = pre * s
        act = silu.astype(BF16).astype(F32)
        weights = vec_ref[2]
        chance = sigmoid(jnp.sum(act * weights, axis=1, keepdims=True))
        gain = gain_col[at, 0:1]
        d_logit = -gain * chance * (1.0 - chance)
        d_pre = d_logit * weights * (s + silu * (1.0 - s))
        d2[at, :] = d_pre.astype(BF16)
        bias_two = bias_two + jnp.sum(d_pre, axis=0, keepdims=True)
        head = head + jnp.sum(d_logit * act, axis=0, keepdims=True)
        value = value + jnp.sum(chance * gain, axis=0, keepdims=True)
        return bias_two, head, value

    zero_row = jnp.zeros((1, hidden), F32)
    bias_two, head, value = lax.fori_loop(
        0, paths // rows_second, second_layer, (zero_row, zero_row, jnp.zeros((1, 1), F32))
    )
    small[17:18, :] = bias_two
    small[18:19, :] = head
    lane = lax.broadcasted_iota(jnp.int32, (1, hidden), 1)
    small[19:20, :] += jnp.where(lane == 0, value, 0.0)
    small[20:24, :] = jnp.zeros((4, hidden), F32)

    def order(step):
        packed = sum(ORDER[chip][step] * 4**chip for chip in range(CHIPS))
        return lax.rem(lax.shift_right_logical(jnp.int32(packed), 2 * c), jnp.int32(4))

    def pair_copy(e):
        return remote(to_pair.at[e], from_pair.at[e], pair_send.at[e], pair_recv.at[e], other)

    def product(step):
        e = order(step)
        rows = pl.ds(pl.multiple_of(e * 2 * depth, 2 * depth), 2 * depth)

        def body(n, carry):
            at = pl.ds(pl.multiple_of(n * tile, tile), tile)
            grads[e, :, at] = jnp.dot(h1t[rows, :], d2[:, at], preferred_element_type=F32)
            return carry

        lax.fori_loop(0, hidden // tile, body, 0)
        theirs = pl.ds(pl.multiple_of((1 - k) * depth, depth), depth)
        to_pair[e] = grads[e, theirs, :].astype(BF16)
        pair_copy(e).start()

    def line_copy(way, e, h, to):
        at = pl.ds(h * part, part)
        return remote(
            to_line.at[e, at, :],
            from_line.at[way, e, at, :],
            line_send.at[e, h],
            line_recv.at[way, e, h],
            to,
        )

    def own_part(e, h):
        mine = pl.ds(pl.multiple_of(k * depth + h * part, part), part)
        return grads[e, mine, :] + from_pair[e, pl.ds(h * part, part), :].astype(F32)

    def along_line(step, halves=range(HALVES)):
        e = order(step)
        if 0 in halves:
            pair_copy(e).wait_recv()
        for h in halves:
            at = pl.ds(h * part, part)

            @pl.when(e > c)
            def _():
                @pl.when(c == 0)
                def _():
                    to_line[e, at, :] = own_part(e, h).astype(BF16)

                @pl.when(c > 0)
                def _():
                    line_copy(0, e, h, other).wait_recv()
                    total = own_part(e, h) + from_line[0, e, at, :].astype(F32)
                    to_line[e, at, :] = total.astype(BF16)

                line_copy(0, e, h, me + 2).start()

            @pl.when(e < c)
            def _():
                @pl.when(c == CHIPS - 1)
                def _():
                    to_line[e, at, :] = own_part(e, h).astype(BF16)

                @pl.when(c < CHIPS - 1)
                def _():
                    line_copy(1, e, h, other).wait_recv()
                    total = own_part(e, h) + from_line[1, e, at, :].astype(F32)
                    to_line[e, at, :] = total.astype(BF16)

                line_copy(1, e, h, me - 2).start()

    product(0)
    product(1)
    pl.when(at_end)(lambda: along_line(0))
    product(2)
    pl.when(at_end)(lambda: along_line(1))
    product(3)
    pl.when(at_end)(lambda: along_line(2))

    def back(m, carry):
        bias_one, first = carry
        at = pl.ds(pl.multiple_of(m * tile, tile), tile)
        d_pre = (
            lax.dot_general(
                d2[at, :], wfull[...], (((1,), (1,)), ((), ())), preferred_element_type=F32
            )
            * slope[at, :]
        )
        bias_one = bias_one + jnp.sum(d_pre, axis=0, keepdims=True)
        first = first + jnp.dot(fac_ref[:, at], d_pre.astype(BF16), preferred_element_type=F32)
        return bias_one, first

    def on_the_way(step, h):
        pl.when(jnp.logical_not(at_end))(lambda: along_line(step, (h,)))

    sums = (zero_row, jnp.zeros((fac_ref.shape[0], hidden), F32))
    sums = lax.fori_loop(0, paths // tile // 2, back, sums)
    on_the_way(0, 0)
    bias_one, first = lax.fori_loop(paths // tile // 2, paths // tile, back, sums)
    small[0:16, :] = first
    small[16:17, :] = bias_one

    my_columns = pl.ds(pl.multiple_of(k * half_columns, half_columns), half_columns)
    their_columns = pl.ds(pl.multiple_of((1 - k) * half_columns, half_columns), half_columns)
    pair_sum = remote(small, small_pair, small_send, small_recv, other)
    pair_sum.start()
    on_the_way(0, 1)
    pair_sum.wait_recv()
    small_chip[c] = small[:, my_columns] + small_pair[:, my_columns]

    def chip_copy(far):
        to = ((c + far) % CHIPS) * 2 + k
        return remote(
            small_chip.at[c], small_chip.at[c], chip_send.at[far - 1], chip_recv.at[c], to
        )

    def chip_landed(far):
        chip = (c + far) % CHIPS
        slot = small_chip.at[chip]
        remote(slot, slot, chip_send.at[far - 1], chip_recv.at[chip], other).wait_recv()

    for far in range(1, CHIPS):
        chip_copy(far).start()
    for h in range(HALVES):
        for step in (1, 2):
            on_the_way(step, h)
    for far in range(1, CHIPS):
        chip_landed(far)
    small_sum[:, my_columns] = small_chip[0] + small_chip[1] + small_chip[2] + small_chip[3]
    mine = small_sum.at[:, my_columns]
    theirs = small_sum.at[:, their_columns]
    share = remote(mine, mine, sum_send, sum_recv, other)
    share.start()

    pair_copy(c).wait_recv()
    for h in range(HALVES):
        mid_ref[pl.ds(h * part, part), :] = own_part(c, h)

    def arrived(way):
        for h in range(HALVES):
            at = pl.ds(h * part, part)
            line_copy(way, c, h, other).wait_recv()
            mid_ref[at, :] += from_line[way, c, at, :].astype(F32)

    pl.when(c > 0)(lambda: arrived(0))
    pl.when(c < CHIPS - 1)(lambda: arrived(1))
    remote(theirs, theirs, sum_send, sum_recv, other).wait_recv()
    small_ref[...] = small_sum[...]

    for back in range(1, dates + 1):
        pl.when(level + back < levels)(level_copy(back).wait_send)
    for h in range(HALVES):
        gather_copy(shard_part(h), me, h, PAIR, other).wait_send()

        @pl.when(c > 0)
        def _():
            gather_copy(shard_part(h), me, h, LEFT, me - 2).wait_send()

        @pl.when(c < CHIPS - 1)
        def _():
            gather_copy(shard_part(h), me, h, RIGHT, me + 2).wait_send()

        for far in range(1, CHIPS):

            @pl.when(c >= far)
            def _():
                slot = me - 2 * far
                source = wfull.at[rows_of(slot, h), :]
                gather_copy(source, slot, h, PAIR, other).wait_send()

                @pl.when(c < CHIPS - 1)
                def _():
                    gather_copy(source, slot, h, RIGHT, me + 2).wait_send()

            @pl.when(c + far < CHIPS)
            def _():
                slot = me + 2 * far
                source = wfull.at[rows_of(slot, h), :]
                gather_copy(source, slot, h, PAIR, other).wait_send()

                @pl.when(c > 0)
                def _():
                    gather_copy(source, slot, h, LEFT, me - 2).wait_send()

    for e in range(CHIPS):
        pair_copy(e).wait_send()
    for step in range(CHIPS - 1):
        for h in range(HALVES):
            line_copy(0, order(step), h, other).wait_send()
    pair_sum.wait_send()
    for far in range(1, CHIPS):
        chip_copy(far).wait_send()
    share.wait_send()


def run_step(level_range, factors, payoff, terminal, decisions, w_first, vectors, shard):
    paths = factors.shape[1]
    dates = payoff.shape[0]
    _, depth, hidden = shard.shape
    part_count = HALVES
    dma = pltpu.SemaphoreType.DMA
    vmem = pl.BlockSpec(memory_space=pltpu.VMEM)
    return pl.pallas_call(
        step_kernel,
        out_shape=(
            jax.ShapeDtypeStruct((depth, hidden), F32),
            jax.ShapeDtypeStruct((24, hidden), F32),
        ),
        in_specs=[pl.BlockSpec(memory_space=pltpu.SMEM)]
        + [pl.BlockSpec(memory_space=pltpu.HBM)] * 7,
        out_specs=(vmem, vmem),
        scratch_shapes=[
            *(
                pltpu.VMEM(a.shape, a.dtype)
                for a in (factors, payoff, terminal, decisions, w_first, vectors, shard)
            ),
            dma((7,)),
            pltpu.VMEM((hidden, hidden), BF16),
            pltpu.VMEM((paths, hidden), BF16),
            pltpu.VMEM((hidden, paths), BF16),
            pltpu.VMEM((paths, hidden), F32),
            pltpu.VMEM((paths, hidden), F32),
            pltpu.VMEM((paths, hidden), BF16),
            pltpu.VMEM((CHIPS, 2 * depth, hidden), F32),
            pltpu.VMEM((CHIPS, depth, hidden), BF16),
            pltpu.VMEM((CHIPS, depth, hidden), BF16),
            pltpu.VMEM((CHIPS, depth, hidden), BF16),
            pltpu.VMEM((2, CHIPS, depth, hidden), BF16),
            pltpu.VMEM((8, paths), F32),
            pltpu.VMEM((dates, 8, paths), F32),
            pltpu.VMEM((paths, 8), F32),
            pltpu.VMEM((24, hidden), F32),
            pltpu.VMEM((24, hidden), F32),
            pltpu.VMEM((CHIPS, 24, hidden // 2), F32),
            pltpu.VMEM((24, hidden), F32),
            dma((dates,)),
            dma((dates,)),
            dma((3, 2 * CHIPS, part_count)),
            dma((2 * CHIPS, part_count)),
            dma((CHIPS,)),
            dma((CHIPS,)),
            dma((CHIPS, part_count)),
            dma((2, CHIPS, part_count)),
            dma,
            dma,
            dma((CHIPS - 1,)),
            dma((CHIPS,)),
            dma,
            dma,
        ],
        compiler_params=pltpu.CompilerParams(
            collective_id=0, has_side_effects=True, vmem_limit_bytes=61 * 2**20
        ),
        cost_estimate=pl.CostEstimate(
            flops=6 * paths * hidden * hidden, bytes_accessed=4 * hidden * hidden, transcendentals=0
        ),
    )(level_range, factors, payoff, terminal, decisions, w_first, vectors, shard)


def update_kernel(
    mid_ref,
    small_ref,
    w_in_ref,
    w_mid_ref,
    vec_ref,
    mom_in_ref,
    mom_mid_ref,
    mom_vec_ref,
    value_ref,
    new_w_in_ref,
    new_w_mid_ref,
    new_vec_ref,
    new_mom_in_ref,
    new_mom_mid_ref,
    new_mom_vec_ref,
    new_in_copy_ref,
    new_mid_copy_ref,
    *,
    paths_total,
):
    value_ref[0] = jnp.sum(small_ref[19:20, :]) / paths_total

    def update(grad, master, momentum, new_master, new_momentum, at):
        moved = MOMENTUM * momentum[0, at, :] + grad
        new_momentum[0, at, :] = moved
        stepped = master[0, at, :] - STEP_SIZE * moved
        new_master[0, at, :] = stepped
        return stepped

    factors = w_in_ref.shape[1]
    everything = pl.ds(0, factors)
    stepped = update(
        small_ref[0:factors, :], w_in_ref, mom_in_ref, new_w_in_ref, new_mom_in_ref, everything
    )
    new_in_copy_ref[0] = stepped.astype(BF16)
    for row in range(vec_ref.shape[0]):
        at_row = small_ref[factors + row : factors + row + 1, :]
        moved = MOMENTUM * mom_vec_ref[row] + at_row
        new_mom_vec_ref[row] = moved
        new_vec_ref[row] = vec_ref[row] - STEP_SIZE * moved
    rows = 16

    def body(i, carry):
        at = pl.ds(pl.multiple_of(i * rows, rows), rows)
        stepped = update(
            mid_ref[at, :], w_mid_ref, mom_mid_ref, new_w_mid_ref, new_mom_mid_ref, at
        )
        new_mid_copy_ref[0, at, :] = stepped.astype(BF16)
        return carry

    lax.fori_loop(0, mid_ref.shape[0] // rows, body, 0)


def shards(
    factors,
    payoff,
    terminal,
    decisions,
    level_range,
    w_in_master,
    w_mid_master,
    vec_master,
    w_in_copy,
    w_mid_copy,
    mom_in,
    mom_mid,
    mom_vec,
):
    paths_total = payoff.shape[1] * lax.axis_size("path")
    vectors = jnp.swapaxes(vec_master, 0, 1)
    mom_rows = jnp.swapaxes(mom_vec, 0, 1)
    mid_grad, small = run_step(
        level_range.T, factors, payoff, terminal, decisions, w_in_copy, vectors, w_mid_copy
    )
    like = jax.ShapeDtypeStruct
    vmem = pl.BlockSpec(memory_space=pltpu.VMEM)
    outs = pl.pallas_call(
        functools.partial(update_kernel, paths_total=paths_total),
        out_shape=(
            like((1,), F32),
            like(w_in_master.shape, F32),
            like(w_mid_master.shape, F32),
            like(vectors.shape, F32),
            like(w_in_master.shape, F32),
            like(w_mid_master.shape, F32),
            like(vectors.shape, F32),
            like(w_in_master.shape, BF16),
            like(w_mid_master.shape, BF16),
        ),
        in_specs=[vmem] * 8,
        out_specs=(pl.BlockSpec(memory_space=pltpu.SMEM),) + (vmem,) * 8,
        compiler_params=pltpu.CompilerParams(vmem_limit_bytes=8 * 2**20),
    )(mid_grad, small, w_in_master, w_mid_master, vectors, mom_in, mom_mid, mom_rows)
    return tuple(jnp.swapaxes(out, 0, 1) if at in (3, 6) else out for at, out in enumerate(outs))


def solution(mesh):
    in_specs = (
        P(None, "path"),
        P(None, "path"),
        P("vol", "path"),
        P(None, "vol", "path"),
        P(),
        P("vol", None, None),
        P("vol", "path", None),
        P("vol", None, None),
        P("vol", None, None),
        P("vol", "path", None),
        P("vol", None, None),
        P("vol", "path", None),
        P("vol", None, None),
    )
    out_specs = (
        P("vol"),
        P("vol", None, None),
        P("vol", "path", None),
        P("vol", None, None),
        P("vol", None, None),
        P("vol", "path", None),
        P("vol", None, None),
        P("vol", None, None),
        P("vol", "path", None),
    )
    return jax.shard_map(shards, mesh=mesh, in_specs=in_specs, out_specs=out_specs, check_vma=False)
```

```python
import functools

import jax
import jax.numpy as jnp
from jax import lax
from jax.experimental import pallas as pl
from jax.experimental.pallas import tpu as pltpu
from jax.sharding import PartitionSpec as P

MOMENTUM = 0.9
STEP_SIZE = 0.01
CHIPS = 4
HALVES = 2
F32 = jnp.float32
BF16 = jnp.bfloat16
ORDER = ((3, 2, 1, 0), (3, 0, 2, 1), (0, 3, 1, 2), (0, 1, 2, 3))


def sigmoid(u):
    return 0.5 * jnp.tanh(0.5 * u) + 0.5


def step_kernel(
    range_ref,
    fac_ref,
    payoff_ref,
    terminal_ref,
    decisions_ref,
    win_ref,
    vec_ref,
    shard_ref,
    mid_ref,
    small_ref,
    wfull,
    h1,
    h1t,
    slope,
    pre2,
    d2,
    grads,
    to_pair,
    from_pair,
    to_line,
    from_line,
    level_out,
    level_in,
    gain_col,
    small,
    small_pair,
    small_chip,
    small_sum,
    level_send,
    level_recv,
    ag_send,
    ag_recv,
    pair_send,
    pair_recv,
    line_send,
    line_recv,
    small_send,
    small_recv,
    chip_send,
    chip_recv,
    sum_send,
    sum_recv,
):
    level = lax.axis_index("vol")
    levels = lax.axis_size("vol")
    dates = payoff_ref.shape[0]
    me = lax.axis_index("path")
    c = me // 2
    k = me % 2
    other = me + 1 - 2 * k
    hidden = h1.shape[1]
    paths = h1.shape[0]
    depth = shard_ref.shape[1]
    part = depth // HALVES
    half_columns = hidden // 2

    def remote(src, dst, send, recv, to):
        return pltpu.make_async_remote_copy(
            src_ref=src,
            dst_ref=dst,
            send_sem=send,
            recv_sem=recv,
            device_id={"path": to},
            device_id_type=pl.DeviceIdType.MESH,
        )

    barrier = pltpu.get_barrier_semaphore()

    def greet_level(to):
        pl.semaphore_signal(
            barrier, inc=1, device_id={"vol": to}, device_id_type=pl.DeviceIdType.MESH
        )

    def each_level(above, below):
        for back in range(1, dates + 1):
            pl.when(level + back < levels)(functools.partial(above, back))
            pl.when(level >= back)(functools.partial(below, back))

    each_level(lambda back: greet_level(level + back), lambda back: greet_level(level - back))
    pl.semaphore_signal(barrier, inc=1, device_id={"path": other}, device_id_type=pl.DeviceIdType.MESH)
    for far in range(1, CHIPS):
        pl.semaphore_signal(
            barrier,
            inc=1,
            device_id={"path": ((c + far) % CHIPS) * 2 + k},
            device_id_type=pl.DeviceIdType.MESH,
        )

    level_out[0:1, :] = terminal_ref[...]
    for date in range(1, dates):
        level_out[date : date + 1, :] = decisions_ref[date - 1].astype(F32)

    def level_copy(back):
        return pltpu.make_async_remote_copy(
            src_ref=level_out,
            dst_ref=level_in.at[back - 1],
            send_sem=level_send.at[back - 1],
            recv_sem=level_recv.at[back - 1],
            device_id={"vol": level + back},
            device_id_type=pl.DeviceIdType.MESH,
        )

    rows_first = 128

    def first_layer(m, carry):
        at = pl.ds(pl.multiple_of(m * rows_first, rows_first), rows_first)
        pre = (
            lax.dot_general(
                fac_ref[:, at], win_ref[0], (((0,), (0,)), ((), ())), preferred_element_type=F32
            )
            + vec_ref[0]
        )
        s = sigmoid(pre)
        act = pre * s
        slope[at, :] = s + act * (1.0 - s)
        h1[at, :] = act.astype(BF16)
        h1t[:, at] = jnp.transpose(act).astype(BF16)
        return carry

    tiles_first = paths // rows_first
    tiles_ahead = tiles_first // 2
    lax.fori_loop(0, tiles_ahead, first_layer, 0)
    peers = CHIPS
    for back in range(1, dates + 1):
        peers = peers + jnp.where(level + back < levels, 1, 0) + jnp.where(level >= back, 1, 0)
    pl.semaphore_wait(barrier, peers)

    def rows_of(slot, h):
        return pl.ds(pl.multiple_of(slot * depth + h * part, part), part)

    LEFT, RIGHT, PAIR = 0, 1, 2

    def gather_copy(source, slot, h, way, to):
        return remote(
            source, wfull.at[rows_of(slot, h), :], ag_send.at[way, slot, h], ag_recv.at[slot, h], to
        )

    def shard_part(h):
        return shard_ref.at[0, pl.ds(h * part, part), :]

    for h in range(HALVES):

        @pl.when(c > 0)
        def _():
            gather_copy(shard_part(h), me, h, LEFT, me - 2).start()

        @pl.when(c < CHIPS - 1)
        def _():
            gather_copy(shard_part(h), me, h, RIGHT, me + 2).start()

    for h in range(HALVES):
        gather_copy(shard_part(h), me, h, PAIR, other).start()
    wfull[pl.ds(pl.multiple_of(me * depth, depth), depth), :] = shard_ref[0]

    def no_level(back):
        level_in[back - 1] = jnp.zeros(level_in.shape[1:], F32)

    for back in range(1, dates + 1):
        pl.when(level + back < levels)(level_copy(back).start)
        pl.when(level < back)(functools.partial(no_level, back))
    lax.fori_loop(tiles_ahead, tiles_first, first_layer, 0)

    def landed(slot, h):
        at = wfull.at[rows_of(slot, h), :]
        gather_copy(at, slot, h, PAIR, other).wait_recv()

    def forward(slot, h, way, to):
        gather_copy(wfull.at[rows_of(slot, h), :], slot, h, way, to).start()

    def relay(far):
        for h in range(HALVES):

            @pl.when(c >= far)
            def _():
                slot = me - 2 * far
                landed(slot, h)

                @pl.when(c < CHIPS - 1)
                def _():
                    forward(slot, h, RIGHT, me + 2)

                forward(slot, h, PAIR, other)

            @pl.when(c + far < CHIPS)
            def _():
                slot = me + 2 * far
                landed(slot, h)

                @pl.when(c > 0)
                def _():
                    forward(slot, h, LEFT, me - 2)

                forward(slot, h, PAIR, other)

    tile = 256

    def middle(chip, first):
        columns = pl.ds(pl.multiple_of(chip * 2 * depth, 2 * depth), 2 * depth)

        def body(m, carry):
            at = pl.ds(pl.multiple_of(m * tile, tile), tile)
            product = jnp.dot(h1[at, columns], wfull[columns, :], preferred_element_type=F32)
            if first:
                pre2[at, :] = product + vec_ref[1]
            else:
                pre2[at, :] += product
            return carry

        lax.fori_loop(0, paths // tile, body, 0)

    def absorb(far):
        @pl.when(c >= far)
        def _():
            for h in range(HALVES):
                landed(other - 2 * far, h)
            middle(c - far, False)

        @pl.when(c + far < CHIPS)
        def _():
            for h in range(HALVES):
                landed(other + 2 * far, h)
            middle(c + far, False)

    at_end = c * (CHIPS - 1 - c) == 0
    relay(1)
    for h in range(HALVES):
        landed(other, h)
    middle(c, True)
    absorb(1)
    relay(2)

    for back in range(1, dates + 1):
        pl.when(level >= back)(level_copy(back).wait_recv)

    def of_level(back, row):
        if back == 0:
            return level_out[row : row + 1, :]
        return level_in[back - 1, row : row + 1, :]

    carry = [of_level(back, 0) for back in range(dates + 1)]
    for date in range(dates - 1, 0, -1):
        lower_end, upper_end = range_ref[0, date], range_ref[1, date]
        after = []
        for back in range(len(carry) - 1):
            here = level - back
            inside = jnp.logical_and(here >= lower_end, here <= upper_end)
            free = jnp.where(inside, of_level(back, date), 0.0)
            taken = jnp.where(here > upper_end, 1.0, free)
            paid = payoff_ref[date : date + 1, :] + carry[back + 1]
            after.append(taken * paid + (1.0 - taken) * carry[back])
        carry = after
    gain_row = payoff_ref[0:1, :] + carry[1] - carry[0]
    active = jnp.logical_and(level >= range_ref[0, 0], level <= range_ref[1, 0])
    rest_row = jnp.where(level > range_ref[1, 0], gain_row, 0.0) + carry[0]
    gain_active = jnp.where(active, gain_row, 0.0)
    gain_col[...] = jnp.transpose(jnp.broadcast_to(gain_active, (8, paths)))
    small[19:20, :] = rest_row
    pl.when(at_end)(lambda: absorb(2))
    relay(3)
    last = (CHIPS - 1) * (1 - c // 2)
    for h in range(HALVES):
        landed(other + 2 * (last - c), h)
    last_columns = pl.ds(pl.multiple_of(last * 2 * depth, 2 * depth), 2 * depth)

    rows_second = 128

    def second_layer(m, carry):
        bias_two, head, value = carry
        at = pl.ds(pl.multiple_of(m * rows_second, rows_second), rows_second)
        pre = pre2[at, :] + jnp.dot(
            h1[at, last_columns], wfull[last_columns, :], preferred_element_type=F32
        )
        s = sigmoid(pre)
        silu = pre * s
        act = silu.astype(BF16).astype(F32)
        weights = vec_ref[2]
        chance = sigmoid(jnp.sum(act * weights, axis=1, keepdims=True))
        gain = gain_col[at, 0:1]
        d_logit = -gain * chance * (1.0 - chance)
        d_pre = d_logit * weights * (s + silu * (1.0 - s))
        d2[at, :] = d_pre.astype(BF16)
        bias_two = bias_two + jnp.sum(d_pre, axis=0, keepdims=True)
        head = head + jnp.sum(d_logit * act, axis=0, keepdims=True)
        value = value + jnp.sum(chance * gain, axis=0, keepdims=True)
        return bias_two, head, value

    zero_row = jnp.zeros((1, hidden), F32)
    bias_two, head, value = lax.fori_loop(
        0, paths // rows_second, second_layer, (zero_row, zero_row, jnp.zeros((1, 1), F32))
    )
    small[17:18, :] = bias_two
    small[18:19, :] = head
    lane = lax.broadcasted_iota(jnp.int32, (1, hidden), 1)
    small[19:20, :] += jnp.where(lane == 0, value, 0.0)
    small[20:24, :] = jnp.zeros((4, hidden), F32)

    def order(step):
        packed = sum(ORDER[chip][step] * 4**chip for chip in range(CHIPS))
        return lax.rem(lax.shift_right_logical(jnp.int32(packed), 2 * c), jnp.int32(4))

    def pair_copy(e):
        return remote(to_pair.at[e], from_pair.at[e], pair_send.at[e], pair_recv.at[e], other)

    def product(step):
        e = order(step)
        rows = pl.ds(pl.multiple_of(e * 2 * depth, 2 * depth), 2 * depth)

        def body(n, carry):
            at = pl.ds(pl.multiple_of(n * tile, tile), tile)
            grads[e, :, at] = jnp.dot(h1t[rows, :], d2[:, at], preferred_element_type=F32)
            return carry

        lax.fori_loop(0, hidden // tile, body, 0)
        theirs = pl.ds(pl.multiple_of((1 - k) * depth, depth), depth)
        to_pair[e] = grads[e, theirs, :].astype(BF16)
        pair_copy(e).start()

    def line_copy(way, e, h, to):
        at = pl.ds(h * part, part)
        return remote(
            to_line.at[e, at, :],
            from_line.at[way, e, at, :],
            line_send.at[e, h],
            line_recv.at[way, e, h],
            to,
        )

    def own_part(e, h):
        mine = pl.ds(pl.multiple_of(k * depth + h * part, part), part)
        return grads[e, mine, :] + from_pair[e, pl.ds(h * part, part), :].astype(F32)

    def along_line(step, halves=range(HALVES)):
        e = order(step)
        if 0 in halves:
            pair_copy(e).wait_recv()
        for h in halves:
            at = pl.ds(h * part, part)

            @pl.when(e > c)
            def _():
                @pl.when(c == 0)
                def _():
                    to_line[e, at, :] = own_part(e, h).astype(BF16)

                @pl.when(c > 0)
                def _():
                    line_copy(0, e, h, other).wait_recv()
                    total = own_part(e, h) + from_line[0, e, at, :].astype(F32)
                    to_line[e, at, :] = total.astype(BF16)

                line_copy(0, e, h, me + 2).start()

            @pl.when(e < c)
            def _():
                @pl.when(c == CHIPS - 1)
                def _():
                    to_line[e, at, :] = own_part(e, h).astype(BF16)

                @pl.when(c < CHIPS - 1)
                def _():
                    line_copy(1, e, h, other).wait_recv()
                    total = own_part(e, h) + from_line[1, e, at, :].astype(F32)
                    to_line[e, at, :] = total.astype(BF16)

                line_copy(1, e, h, me - 2).start()

    product(0)
    product(1)
    pl.when(at_end)(lambda: along_line(0))
    product(2)
    pl.when(at_end)(lambda: along_line(1))
    product(3)
    pl.when(at_end)(lambda: along_line(2))

    def back(m, carry):
        bias_one, first = carry
        at = pl.ds(pl.multiple_of(m * tile, tile), tile)
        d_pre = (
            lax.dot_general(
                d2[at, :], wfull[...], (((1,), (1,)), ((), ())), preferred_element_type=F32
            )
            * slope[at, :]
        )
        bias_one = bias_one + jnp.sum(d_pre, axis=0, keepdims=True)
        first = first + jnp.dot(fac_ref[:, at], d_pre.astype(BF16), preferred_element_type=F32)
        return bias_one, first

    def on_the_way(step, h):
        pl.when(jnp.logical_not(at_end))(lambda: along_line(step, (h,)))

    sums = (zero_row, jnp.zeros((fac_ref.shape[0], hidden), F32))
    sums = lax.fori_loop(0, paths // tile // 2, back, sums)
    on_the_way(0, 0)
    bias_one, first = lax.fori_loop(paths // tile // 2, paths // tile, back, sums)
    small[0:16, :] = first
    small[16:17, :] = bias_one

    my_columns = pl.ds(pl.multiple_of(k * half_columns, half_columns), half_columns)
    their_columns = pl.ds(pl.multiple_of((1 - k) * half_columns, half_columns), half_columns)
    pair_sum = remote(small, small_pair, small_send, small_recv, other)
    pair_sum.start()
    on_the_way(0, 1)
    pair_sum.wait_recv()
    small_chip[c] = small[:, my_columns] + small_pair[:, my_columns]

    def chip_copy(far):
        to = ((c + far) % CHIPS) * 2 + k
        return remote(
            small_chip.at[c], small_chip.at[c], chip_send.at[far - 1], chip_recv.at[c], to
        )

    def chip_landed(far):
        chip = (c + far) % CHIPS
        slot = small_chip.at[chip]
        remote(slot, slot, chip_send.at[far - 1], chip_recv.at[chip], other).wait_recv()

    for far in range(1, CHIPS):
        chip_copy(far).start()
    for h in range(HALVES):
        for step in (1, 2):
            on_the_way(step, h)
    for far in range(1, CHIPS):
        chip_landed(far)
    small_sum[:, my_columns] = small_chip[0] + small_chip[1] + small_chip[2] + small_chip[3]
    mine = small_sum.at[:, my_columns]
    theirs = small_sum.at[:, their_columns]
    share = remote(mine, mine, sum_send, sum_recv, other)
    share.start()

    pair_copy(c).wait_recv()
    for h in range(HALVES):
        mid_ref[pl.ds(h * part, part), :] = own_part(c, h)

    def arrived(way):
        for h in range(HALVES):
            at = pl.ds(h * part, part)
            line_copy(way, c, h, other).wait_recv()
            mid_ref[at, :] += from_line[way, c, at, :].astype(F32)

    pl.when(c > 0)(lambda: arrived(0))
    pl.when(c < CHIPS - 1)(lambda: arrived(1))
    remote(theirs, theirs, sum_send, sum_recv, other).wait_recv()
    small_ref[...] = small_sum[...]

    for back in range(1, dates + 1):
        pl.when(level + back < levels)(level_copy(back).wait_send)
    for h in range(HALVES):
        gather_copy(shard_part(h), me, h, PAIR, other).wait_send()

        @pl.when(c > 0)
        def _():
            gather_copy(shard_part(h), me, h, LEFT, me - 2).wait_send()

        @pl.when(c < CHIPS - 1)
        def _():
            gather_copy(shard_part(h), me, h, RIGHT, me + 2).wait_send()

        for far in range(1, CHIPS):

            @pl.when(c >= far)
            def _():
                slot = me - 2 * far
                source = wfull.at[rows_of(slot, h), :]
                gather_copy(source, slot, h, PAIR, other).wait_send()

                @pl.when(c < CHIPS - 1)
                def _():
                    gather_copy(source, slot, h, RIGHT, me + 2).wait_send()

            @pl.when(c + far < CHIPS)
            def _():
                slot = me + 2 * far
                source = wfull.at[rows_of(slot, h), :]
                gather_copy(source, slot, h, PAIR, other).wait_send()

                @pl.when(c > 0)
                def _():
                    gather_copy(source, slot, h, LEFT, me - 2).wait_send()

    for e in range(CHIPS):
        pair_copy(e).wait_send()
    for step in range(CHIPS - 1):
        for h in range(HALVES):
            line_copy(0, order(step), h, other).wait_send()
    pair_sum.wait_send()
    for far in range(1, CHIPS):
        chip_copy(far).wait_send()
    share.wait_send()


def run_step(level_range, factors, payoff, terminal, decisions, w_first, vectors, shard):
    paths = factors.shape[1]
    dates = payoff.shape[0]
    _, depth, hidden = shard.shape
    part_count = HALVES
    dma = pltpu.SemaphoreType.DMA
    vmem = pl.BlockSpec(memory_space=pltpu.VMEM)
    return pl.pallas_call(
        step_kernel,
        out_shape=(
            jax.ShapeDtypeStruct((depth, hidden), F32),
            jax.ShapeDtypeStruct((24, hidden), F32),
        ),
        in_specs=[pl.BlockSpec(memory_space=pltpu.SMEM)] + [vmem] * 7,
        out_specs=(vmem, vmem),
        scratch_shapes=[
            pltpu.VMEM((hidden, hidden), BF16),
            pltpu.VMEM((paths, hidden), BF16),
            pltpu.VMEM((hidden, paths), BF16),
            pltpu.VMEM((paths, hidden), F32),
            pltpu.VMEM((paths, hidden), F32),
            pltpu.VMEM((paths, hidden), BF16),
            pltpu.VMEM((CHIPS, 2 * depth, hidden), F32),
            pltpu.VMEM((CHIPS, depth, hidden), BF16),
            pltpu.VMEM((CHIPS, depth, hidden), BF16),
            pltpu.VMEM((CHIPS, depth, hidden), BF16),
            pltpu.VMEM((2, CHIPS, depth, hidden), BF16),
            pltpu.VMEM((8, paths), F32),
            pltpu.VMEM((dates, 8, paths), F32),
            pltpu.VMEM((paths, 8), F32),
            pltpu.VMEM((24, hidden), F32),
            pltpu.VMEM((24, hidden), F32),
            pltpu.VMEM((CHIPS, 24, hidden // 2), F32),
            pltpu.VMEM((24, hidden), F32),
            dma((dates,)),
            dma((dates,)),
            dma((3, 2 * CHIPS, part_count)),
            dma((2 * CHIPS, part_count)),
            dma((CHIPS,)),
            dma((CHIPS,)),
            dma((CHIPS, part_count)),
            dma((2, CHIPS, part_count)),
            dma,
            dma,
            dma((CHIPS - 1,)),
            dma((CHIPS,)),
            dma,
            dma,
        ],
        compiler_params=pltpu.CompilerParams(collective_id=0, has_side_effects=True),
        cost_estimate=pl.CostEstimate(
            flops=6 * paths * hidden * hidden, bytes_accessed=4 * hidden * hidden, transcendentals=0
        ),
    )(level_range, factors, payoff, terminal, decisions, w_first, vectors, shard)


def update_kernel(
    mid_ref,
    small_ref,
    w_in_ref,
    w_mid_ref,
    vec_ref,
    mom_in_ref,
    mom_mid_ref,
    mom_vec_ref,
    value_ref,
    new_w_in_ref,
    new_w_mid_ref,
    new_vec_ref,
    new_mom_in_ref,
    new_mom_mid_ref,
    new_mom_vec_ref,
    new_in_copy_ref,
    new_mid_copy_ref,
    *,
    paths_total,
):
    def update(grad, master, momentum, new_master, new_momentum, at):
        moved = MOMENTUM * momentum[0, at, :] + grad
        new_momentum[0, at, :] = moved
        stepped = master[0, at, :] - STEP_SIZE * moved
        new_master[0, at, :] = stepped
        return stepped

    @pl.when(pl.program_id(0) == 0)
    def _():
        value_ref[0] = jnp.sum(small_ref[19:20, :]) / paths_total
        factors = w_in_ref.shape[1]
        everything = pl.ds(0, factors)
        stepped = update(
            small_ref[0:factors, :], w_in_ref, mom_in_ref, new_w_in_ref, new_mom_in_ref, everything
        )
        new_in_copy_ref[0] = stepped.astype(BF16)
        for row in range(vec_ref.shape[0]):
            at_row = small_ref[factors + row : factors + row + 1, :]
            moved = MOMENTUM * mom_vec_ref[row] + at_row
            new_mom_vec_ref[row] = moved
            new_vec_ref[row] = vec_ref[row] - STEP_SIZE * moved

    rows = 16

    def body(i, carry):
        at = pl.ds(pl.multiple_of(i * rows, rows), rows)
        stepped = update(
            mid_ref[at, :], w_mid_ref, mom_mid_ref, new_w_mid_ref, new_mom_mid_ref, at
        )
        new_mid_copy_ref[0, at, :] = stepped.astype(BF16)
        return carry

    lax.fori_loop(0, mid_ref.shape[0] // rows, body, 0)


def shards(
    factors,
    payoff,
    terminal,
    decisions,
    level_range,
    w_in_master,
    w_mid_master,
    vec_master,
    w_in_copy,
    w_mid_copy,
    mom_in,
    mom_mid,
    mom_vec,
):
    paths_total = payoff.shape[1] * lax.axis_size("path")
    vectors = jnp.swapaxes(vec_master, 0, 1)
    mom_rows = jnp.swapaxes(mom_vec, 0, 1)
    mid_grad, small = run_step(
        level_range.T, factors, payoff, terminal, decisions, w_in_copy, vectors, w_mid_copy
    )
    like = jax.ShapeDtypeStruct
    steps = 4
    depth, hidden = mid_grad.shape

    def whole(array):
        return pl.BlockSpec(array.shape, lambda i: (0,) * array.ndim)

    block = pl.BlockSpec((1, depth // steps, hidden), lambda i: (0, i, 0))
    outs = pl.pallas_call(
        functools.partial(update_kernel, paths_total=paths_total),
        out_shape=(
            like((1,), F32),
            like(w_in_master.shape, F32),
            like(w_mid_master.shape, F32),
            like(vectors.shape, F32),
            like(w_in_master.shape, F32),
            like(w_mid_master.shape, F32),
            like(vectors.shape, F32),
            like(w_in_master.shape, BF16),
            like(w_mid_master.shape, BF16),
        ),
        grid=(steps,),
        in_specs=[
            pl.BlockSpec((depth // steps, hidden), lambda i: (i, 0)),
            whole(small),
            whole(w_in_master),
            block,
            whole(vectors),
            whole(mom_in),
            block,
            whole(mom_rows),
        ],
        out_specs=(
            pl.BlockSpec(memory_space=pltpu.SMEM),
            whole(w_in_master),
            block,
            whole(vectors),
            whole(w_in_master),
            block,
            whole(vectors),
            whole(w_in_master),
            block,
        ),
    )(mid_grad, small, w_in_master, w_mid_master, vectors, mom_in, mom_mid, mom_rows)
    return tuple(jnp.swapaxes(out, 0, 1) if at in (3, 6) else out for at, out in enumerate(outs))


def solution(mesh):
    in_specs = (
        P(None, "path"),
        P(None, "path"),
        P("vol", "path"),
        P(None, "vol", "path"),
        P(),
        P("vol", None, None),
        P("vol", "path", None),
        P("vol", None, None),
        P("vol", None, None),
        P("vol", "path", None),
        P("vol", None, None),
        P("vol", "path", None),
        P("vol", None, None),
    )
    out_specs = (
        P("vol"),
        P("vol", None, None),
        P("vol", "path", None),
        P("vol", None, None),
        P("vol", None, None),
        P("vol", "path", None),
        P("vol", None, None),
        P("vol", None, None),
        P("vol", "path", None),
    )
    return jax.shard_map(shards, mesh=mesh, in_specs=in_specs, out_specs=out_specs, check_vma=False)
```
